32 devices in a mesh: groups: 2 (over y), branch: 2 (over core), tok: 8 (over z, x).
Axes of the slice: x: 2, y: 2, z: 4, core: 2. Of those that a mesh axis runs over, the one named last changes fastest.
Arguments:
- queries: bfloat16 [512, 4096], P(('groups', 'tok')), parts along dimension 0, may hold values from -8 to 8
- keys: bfloat16 [512, 4096], P(('groups', 'tok')), parts along dimension 0, may hold values from -8 to 8
- values: bfloat16 [512, 4096], P(('groups', 'tok')), parts along dimension 0, may hold values from -6 to 6
- keyboard: int32 [16], P('groups'), parts along dimension 0, may hold values from 0 to 15
- mouse: int32 [16], P('groups'), parts along dimension 0, may hold values from 0 to 31
- key_table: bfloat16 [16, 2, 4096], replicated, may hold values from -3 to 3
- mouse_table: bfloat16 [32, 2, 4096], replicated, may hold values from -3 to 3
- guidance: float32 [4], replicated, may hold values from 0.5 to 1.5
- out_weight: bfloat16 [4096, 64], replicated, may hold values from -0.09375 to 0.09375
- latent: float32 [512, 64], P(('groups', 'tok')), parts along dimension 0, may hold values from -6 to 6
- conv_in: bfloat16 [3, 3, 16, 384], replicated, may hold values from -0.5 to 0.5
- gain: float32 [384], replicated, may hold values from 0.5 to 1.5
- conv_out: bfloat16 [3, 3, 384, 3], replicated, may hold values from -0.109375 to 0.109375
Outputs:
- velocity: float32 [512, 64], P(('groups', 'tok')), parts along dimension 0
- frames_rgb: float32 [3, 32, 64], P(None, ('groups', 'tok')), parts along dimension 1
The draws below stay inside these ranges and needn't reach their ends.
There are 2 independent parts, one for each index of `groups`. The reference program is written for one: setup_inputs(seed, part) draws one part's arguments, and reference() takes and returns one part's arrays. A program takes and returns all parts, laid end to end along the dimension named above; an argument that names none is the same for every part. Nothing has to cross between parts.
All inputs are finite; a program needn't handle non-finite values.
Results may differ from the reference program's by a relative error of at most 0.012.
Values may be sent and summed in bfloat16 or wider, within the bound.
A program may use at most 64 MiB of HBM per device.

```python
import jax
import jax.numpy as jnp
from jax import lax

HEAD_DIM = 128
HEADS = 32
D = 4096
TOK_DEV = 32
TOKENS = 256
FRAMES = 8
LAT_CH = 16
PATCH_CH = 64
DEC = 384
KEYS = 16
MOUSE = 32
BRANCHES = 4
N_TOK = 8


def base_field(key):
    field = 1.5 * jax.random.normal(jax.random.fold_in(key, 6), (TOKENS, D))
    return jnp.clip(field, -8.0, 8.0)


def draw_queries(key, part):
    field = base_field(jax.random.fold_in(key, 101))
    return field.astype(jnp.bfloat16)


def draw_keys(key, part):
    field = base_field(jax.random.fold_in(key, 202))
    return field.astype(jnp.bfloat16)


def with_ends(result, own_key, smallest, top_value):
    dims = result.shape
    index_at = [jax.random.randint(jax.random.fold_in(own_key, axis), (), 0, dims[axis]) for axis in range(len(dims))]
    result = result.at[tuple(index_at)].set(smallest)
    longest = dims.index(max(dims))
    index_at[longest] = (index_at[longest] + 1) % dims[longest]
    return result.at[tuple(index_at)].set(top_value)


def levels(key, extent, cuts, low, high):
    factor_of, own = 1.0, jax.random.fold_in(key, 6)
    for axis_at, parts in cuts:
        heights = jnp.exp(jax.random.uniform(jax.random.fold_in(own, axis_at), (parts,), jnp.float32, low / len(cuts), high / len(cuts)))
        factor_of = factor_of * jnp.repeat(heights, extent[axis_at] // parts).reshape([-1 if axis == axis_at else 1 for axis in range(len(extent))])
    return factor_of


def scatter_about(key, extent, width, bound, shards=(), kind=jnp.bfloat16):
    drawn = jax.random.normal(key, extent, jnp.float32) * width
    if len(shards) > 0:
        drawn = levels(key, extent, shards, -0.22, 0.18) * drawn
    return jnp.clip(drawn, min=-bound, max=bound).astype(kind)


def setup_inputs(seed: int = 0, part: int = 0) -> dict:
    key_list = jax.random.split(jax.random.key(seed), 14)
    part_splits = jax.random.split(jax.random.fold_in(key_list[13], part), 14)
    return {
        "queries": draw_queries(jax.random.fold_in(jax.random.fold_in(key_list[13], part), 71), part),
        "keys": draw_keys(jax.random.fold_in(jax.random.fold_in(key_list[13], part), 71), part),
        "values": scatter_about(part_splits[2], (TOKENS, D), 1.0, 6.0, ((0, 8),)),
        "keyboard": with_ends(jax.random.randint(part_splits[3], (FRAMES,), 0, KEYS), jax.random.fold_in(part_splits[3], 1), 0, KEYS - 1).astype(jnp.int32),
        "mouse": with_ends(jax.random.randint(part_splits[4], (FRAMES,), 0, MOUSE), jax.random.fold_in(part_splits[4], 1), 0, MOUSE - 1).astype(jnp.int32),
        "key_table": scatter_about(key_list[5], (KEYS, 2, D), 0.5, 3.0),
        "mouse_table": scatter_about(key_list[6], (MOUSE, 2, D), 0.5, 3.0),
        "guidance": jnp.clip(jax.random.uniform(key_list[7], (BRANCHES,), jnp.float32, 0.5, 1.5), 0.5, 1.5),
        "out_weight": scatter_about(key_list[8], (D, PATCH_CH), D ** -0.5, 0.09375),
        "latent": scatter_about(part_splits[9], (TOKENS, PATCH_CH), 1.0, 6.0, ((0, 8),), jnp.float32),
        "conv_in": scatter_about(key_list[10], (3, 3, LAT_CH, DEC), (9 * LAT_CH) ** -0.5, 0.5),
        "gain": jnp.clip(1.0 + 0.1 * jax.random.normal(key_list[11], (DEC,), jnp.float32), 0.5, 1.5),
        "conv_out": scatter_about(key_list[12], (3, 3, DEC, 3), (9 * DEC) ** -0.5, 0.109375),
    }


step_size = 0.25
norm_eps = 1e-06
branch_flags = ((1.0, 1.0), (0.0, 1.0), (1.0, 0.0), (0.0, 0.0))

def action_terms(keyboard, mouse, key_table, mouse_table, flag_key, flag_mouse):
    pick_key = (keyboard[:, None] == jnp.arange(KEYS, dtype=jnp.int32)[None, :]).astype(jnp.float32)
    pick_mouse = (mouse[:, None] == jnp.arange(MOUSE, dtype=jnp.int32)[None, :]).astype(jnp.float32)
    rows_key = jnp.einsum('fk,kcd->fcd', pick_key, key_table.astype(jnp.float32))
    rows_mouse = jnp.einsum('fk,kcd->fcd', pick_mouse, mouse_table.astype(jnp.float32))
    return flag_key * rows_key + flag_mouse * rows_mouse

def convolve(padded, weight):
    rows = padded.shape[1] - 2
    cols = padded.shape[2] - 2
    total = jnp.zeros((padded.shape[0], rows, cols, weight.shape[-1]), jnp.float32)
    for first in range(3):
        for second in range(3):
            window = padded[:, first:first + rows, second:second + cols, :].astype(jnp.float32)
            total = total + jnp.einsum('frci,io->frco', window, weight[first, second].astype(jnp.float32))
    return total

def reference(queries, keys, values, keyboard, mouse, key_table, mouse_table, guidance, out_weight, latent, conv_in, gain, conv_out):
    frame_tok = TOKENS // FRAMES
    terms = jnp.stack([action_terms(keyboard, mouse, key_table, mouse_table, branch_flags[b][0], branch_flags[b][1]) for b in range(BRANCHES)])
    key_bias = terms[:, :, 0].astype(jnp.bfloat16)
    value_term = terms[:, :, 1]
    key_bias = key_bias.reshape(BRANCHES, FRAMES, HEADS, HEAD_DIM).transpose(2, 0, 1, 3)
    value_term = value_term.reshape(BRANCHES, FRAMES, HEADS, HEAD_DIM).transpose(2, 0, 1, 3)
    head_queries = queries.reshape(TOKENS, HEADS, HEAD_DIM).transpose(1, 0, 2)
    head_keys = keys.reshape(TOKENS, HEADS, HEAD_DIM).transpose(1, 0, 2)
    head_values = values.reshape(TOKENS, HEADS, HEAD_DIM).transpose(1, 0, 2)

    def one_head(inputs):
        head_q, head_k, head_v, head_bias, head_term = inputs
        base = jnp.dot(head_q, head_k.T, preferred_element_type=jnp.float32)
        grouped = base.reshape(TOKENS, FRAMES, frame_tok)
        combined = jnp.zeros((TOKENS, HEAD_DIM), jnp.float32)
        for branch in range(BRANCHES):
            frame_scores = jnp.dot(head_q, head_bias[branch].T, preferred_element_type=jnp.float32)
            scores = (grouped + frame_scores[:, :, None]).reshape(TOKENS, TOKENS) * HEAD_DIM ** (-0.5)
            top = lax.optimization_barrier(jnp.max(scores, axis=-1, keepdims=True))
            raised = jnp.exp(scores - top)
            total = lax.optimization_barrier(jnp.sum(raised, axis=-1))
            shifted = head_v.astype(jnp.float32).reshape(FRAMES, frame_tok, HEAD_DIM) + head_term[branch][:, None, :]
            shifted = shifted.reshape(TOKENS, HEAD_DIM).astype(jnp.bfloat16)
            summed = jnp.dot(raised.astype(jnp.bfloat16), shifted, preferred_element_type=jnp.float32)
            attended = (summed / total[:, None]).astype(jnp.bfloat16)
            combined = combined + guidance[branch] * attended.astype(jnp.float32)
        return combined
    per_head = lax.map(one_head, (head_queries, head_keys, head_values, key_bias, value_term))
    combined = per_head.transpose(1, 0, 2).reshape(TOKENS, HEADS * HEAD_DIM).astype(jnp.bfloat16)
    velocity = jnp.dot(combined, out_weight, preferred_element_type=jnp.float32)
    stepped = latent - step_size * velocity
    patch_rows = N_TOK // FRAMES
    grid = stepped.reshape(FRAMES, patch_rows, TOK_DEV, 2, 2, LAT_CH).transpose(0, 1, 3, 2, 4, 5)
    grid = grid.reshape(1, FRAMES * 2 * patch_rows, 2 * TOK_DEV, LAT_CH).astype(jnp.bfloat16)
    padded = jnp.pad(grid, ((0, 0), (1, 1), (1, 1), (0, 0)))
    features = convolve(padded, conv_in)
    scaled = features * lax.rsqrt(lax.optimization_barrier(jnp.mean(features * features, axis=-1, keepdims=True)) + norm_eps) * gain
    normed = jax.nn.silu(scaled).astype(jnp.bfloat16)
    colours = convolve(jnp.pad(normed, ((0, 0), (1, 1), (1, 1), (0, 0))), conv_out)
    frames_rgb = colours.transpose(3, 0, 1, 2).reshape(3, FRAMES * 2 * patch_rows, 2 * TOK_DEV)
    return (velocity, frames_rgb)
```

```python
import functools
import math

import jax
import jax.numpy as jnp
from jax import lax
from jax.experimental import pallas as pl
from jax.experimental.pallas import tpu as pltpu
from jax.sharding import PartitionSpec as P

MESH = pl.DeviceIdType.MESH

HEAD_DIM = 128


step_size = 0.25
norm_eps = 1e-06


def passed_along(value, axis, steps):
    count = lax.axis_size(axis)
    pairs = [(source, (source + steps) % count) for source in range(count)]
    return lax.ppermute(value, axis, pairs)


def with_halo(block, sides, width):
    for axis, dim in sides:
        count = lax.axis_size(axis)
        forward = [(i, i + 1) for i in range(count - 1)]
        backward = [(target, source) for source, target in forward]
        low = lax.ppermute(
            lax.slice_in_dim(block, block.shape[dim] - width, None, axis=dim), axis, forward
        )
        high = lax.ppermute(lax.slice_in_dim(block, 0, width, axis=dim), axis, backward)
        block = jnp.concatenate([low, block, high], axis=dim)
    return block


def action_terms(keyboard, mouse, key_table, mouse_table, branch):
    flag_key = jnp.where(branch % 2 == 0, 1.0, 0.0).astype(jnp.float32)
    flag_mouse = jnp.where(branch < 2, 1.0, 0.0).astype(jnp.float32)
    pick_key = (
        keyboard[:, None] == jnp.arange(key_table.shape[0], dtype=jnp.int32)[None, :]
    ).astype(jnp.bfloat16)
    pick_mouse = (
        mouse[:, None] == jnp.arange(mouse_table.shape[0], dtype=jnp.int32)[None, :]
    ).astype(jnp.bfloat16)
    rows_key = jnp.einsum("fk,kcd->fcd", pick_key, key_table, preferred_element_type=jnp.float32)
    rows_mouse = jnp.einsum(
        "fk,kcd->fcd", pick_mouse, mouse_table, preferred_element_type=jnp.float32
    )
    return flag_key * rows_key + flag_mouse * rows_mouse


def pick_heads(array, first, taken, sets):
    lead = array.shape[:-1]
    split = array.reshape(lead + (sets, -1, HEAD_DIM))
    kept = lax.dynamic_slice_in_dim(split, first, taken, len(lead) + 1)
    return kept.reshape(lead + (sets * taken * HEAD_DIM,))


def heads_layout(array, rounds, sets):
    rows, width = array.shape
    piece = rows // rounds
    grouped = array.reshape(rounds, piece, sets, width // sets)
    return grouped.transpose(0, 2, 1, 3).reshape(rows * sets, width // sets)


def tokens_layout(array, rounds, sets):
    rows, width = array.shape
    piece = rows // (rounds * sets)
    grouped = array.reshape(rounds, sets, piece, width)
    return grouped.transpose(0, 2, 1, 3).reshape(rounds * piece, sets * width)


def attend(local_q, local_k, local_v, key_bias, value_term, rounds, sets):
    rows, width = local_q.shape
    heads_here = width // HEAD_DIM
    count_branches = key_bias.shape[0]
    frames = key_bias.shape[1]
    block = rows // frames
    scale = HEAD_DIM ** (-0.5)
    query = local_q.reshape(rows, heads_here, HEAD_DIM)
    bias_heads = key_bias.reshape(count_branches, frames, heads_here, HEAD_DIM)
    frame_scores = jnp.einsum(
        "qhd,bfhd->bhqf", query, bias_heads, preferred_element_type=jnp.float32
    )

    def visit(block_keys, block_values, carry):
        top, total, summed = carry
        base = jnp.einsum(
            "qhd,khd->hqk",
            query,
            block_keys.reshape(rows, heads_here, HEAD_DIM),
            preferred_element_type=jnp.float32,
        )
        grouped = base.reshape(heads_here, rows, frames, block)
        plain_values = block_values.astype(jnp.float32).reshape(frames, block, width)
        tops, totals, sums = ([], [], [])
        for which in range(count_branches):
            scores = (grouped + frame_scores[which][..., None]).reshape(
                heads_here, rows, rows
            ) * scale
            fresh = jnp.maximum(top[which], jnp.max(scores, axis=-1))
            shrink = jnp.exp(top[which] - fresh)
            raised = jnp.exp(scores - fresh[..., None])
            shifted = (plain_values + value_term[which][:, None, :]).astype(jnp.bfloat16)
            shifted = shifted.reshape(rows, heads_here, HEAD_DIM)
            product = jnp.einsum(
                "hqk,khd->hqd",
                raised.astype(jnp.bfloat16),
                shifted,
                preferred_element_type=jnp.float32,
            )
            tops.append(fresh)
            totals.append(total[which] * shrink + jnp.sum(raised, axis=-1))
            sums.append(summed[which] * shrink[..., None] + product)
        return (jnp.stack(tops), jnp.stack(totals), jnp.stack(sums))

    start = (
        jnp.full((count_branches, heads_here, rows), -jnp.inf, jnp.float32),
        jnp.zeros((count_branches, heads_here, rows), jnp.float32),
        jnp.zeros((count_branches, heads_here, rows, HEAD_DIM), jnp.float32),
    )
    carry = visit(local_k, local_v, start)

    def turn(step, state):
        block_keys, block_values, inner = state
        block_keys, block_values = passed_along((block_keys, block_values), "tok", sets)
        return (block_keys, block_values, visit(block_keys, block_values, inner))

    _, _, carry = lax.fori_loop(0, rounds - 1, turn, (local_k, local_v, carry))
    _, total, summed = carry
    attended = (summed / total[..., None]).astype(jnp.bfloat16)
    return attended.transpose(0, 2, 1, 3).reshape(count_branches, rows, heads_here * HEAD_DIM)


def clear_rows(array, depth, top_edge, bottom_edge):
    height = array.shape[0]
    place = jnp.arange(height, dtype=jnp.int32)
    drop = (place < depth) & top_edge | (place >= height - depth) & bottom_edge
    return jnp.where(drop[:, None, None], jnp.zeros_like(array), array)


def convolve(array, weight):
    rows = array.shape[0] - 2
    cols = array.shape[1]
    padded = jnp.pad(array, ((0, 0), (1, 1), (0, 0)))
    total = jnp.zeros((rows, cols, weight.shape[-1]), jnp.float32)
    for first in range(3):
        for second in range(3):
            window = padded[first : first + rows, second : second + cols, :]
            total = total + jnp.einsum(
                "rci,io->rco", window, weight[first, second], preferred_element_type=jnp.float32
            )
    return total


def normalize(features, gain):
    scaled = (
        features
        * lax.rsqrt(jnp.mean(features * features, axis=-1, keepdims=True) + norm_eps)
        * gain
    )
    return jax.nn.silu(scaled).astype(jnp.bfloat16)


def shards(
    queries,
    keys,
    values,
    keyboard,
    mouse,
    key_table,
    mouse_table,
    guidance,
    out_weight,
    latent,
    conv_in,
    gain,
    conv_out,
):
    count = lax.axis_size("tok")
    index = lax.axis_index("tok")
    branch = lax.axis_index("branch")
    sets = 8
    rounds = count // sets
    group = index % sets
    tok_dev, width = queries.shape
    per_group = width // (sets * HEAD_DIM)
    taken = per_group // 2
    first = branch * taken
    branches = [0, 1, 2, 3]
    spread_q = heads_layout(pick_heads(queries, first, taken, sets), rounds, sets)
    spread_k = heads_layout(pick_heads(keys, first, taken, sets), rounds, sets)
    spread_v = heads_layout(pick_heads(values, first, taken, sets), rounds, sets)
    local_q, local_k, local_v = (
        lax.all_to_all(spread_q, "tok", split_axis=0, concat_axis=0, tiled=True),
        lax.all_to_all(spread_k, "tok", split_axis=0, concat_axis=0, tiled=True),
        lax.all_to_all(spread_v, "tok", split_axis=0, concat_axis=0, tiled=True),
    )
    terms = jnp.stack(
        [action_terms(keyboard, mouse, key_table, mouse_table, which) for which in branches]
    )
    mine = pick_heads(terms, first, taken, sets)
    mine = mine.reshape(mine.shape[:-1] + (sets, -1))
    mine = lax.dynamic_index_in_dim(mine, group, 3, keepdims=False)
    key_bias = mine[:, :, 0].astype(jnp.bfloat16)
    value_term = mine[:, :, 1]
    outputs = attend(local_q, local_k, local_v, key_bias, value_term, rounds, sets)
    factors = [guidance[which] for which in branches]
    partial_value = factors[0] * outputs[0].astype(jnp.float32)
    for which in range(1, len(branches)):
        partial_value = partial_value + factors[which] * outputs[which].astype(jnp.float32)
    returned = lax.all_to_all(
        partial_value.astype(jnp.bfloat16), "tok", split_axis=0, concat_axis=0, tiled=True
    )
    split_weight = out_weight.reshape(sets, per_group, HEAD_DIM, -1)
    rows_weight = lax.dynamic_slice_in_dim(split_weight, first, taken, 1).reshape(
        sets * taken * HEAD_DIM, -1
    )
    projected = jnp.dot(
        tokens_layout(returned, rounds, sets), rows_weight, preferred_element_type=jnp.float32
    )
    velocity = lax.psum(projected, "branch")
    stepped = latent - step_size * velocity
    grid = (
        stepped.reshape(tok_dev, 2, 2, -1)
        .transpose(1, 0, 2, 3)
        .reshape(2, 2 * tok_dev, -1)
        .astype(jnp.bfloat16)
    )
    top_edge = index == 0
    bottom_edge = index == count - 1
    bordered = with_halo(grid, (("tok", 0),), 1)
    bordered = clear_rows(bordered, 1, top_edge, bottom_edge)
    hidden = normalize(convolve(bordered, conv_in), gain)
    hidden = with_halo(hidden, (("tok", 0),), 1)
    hidden = clear_rows(hidden, 1, top_edge, bottom_edge)
    colours = convolve(hidden, conv_out)
    return (velocity, colours.transpose(2, 0, 1))


def contract_last(left, right):
    return lax.dot_general(
        left, right, (((1,), (1,)), ((), ())), preferred_element_type=jnp.float32
    )


def fused(
    count,
    kb_s, ms_s, guide_s,
    q_hbm, k_hbm, v_hbm, kt_hbm, mt_hbm, ow_hbm, lat_hbm, ci_hbm, gain_hbm, co_hbm,
    vel_out, rgb_out,
    qs, ks, vs, rq, rk, rv, kt, mt, ow, lat, ci, gain, co,
    act, kbias, wts, psend, precv, ext, late, wbig, vt, weave,
    local_sem, send_sem, recv_sem, send2, recv2, lat_send, lat_recv, x_send, x_recv,
):
    me = lax.axis_index("tok")
    core = lax.axis_index("branch")
    other = 1 - core
    rows = q_hbm.shape[0]
    half = rows // 2
    cols = rq.shape[1]
    heads = cols // HEAD_DIM
    tokens = rows * count
    patch = lat_hbm.shape[1]
    dec = gain.shape[0]
    lat_ch = ci.shape[0] // 9
    below = lax.rem(me + count - 1, count)
    above = lax.rem(me + 1, count)
    has_low = me > 0
    has_high = me < count - 1

    def span(index):
        return pl.ds(pl.multiple_of((2 * index + core) * cols, cols), cols)

    def own_rows(index):
        return pl.ds(pl.multiple_of(index * rows, rows), rows)

    ext[...] = jnp.zeros_like(ext)
    late[0] = jnp.zeros(late.shape[1:], late.dtype)
    late[2] = jnp.zeros(late.shape[1:], late.dtype)
    barrier = pltpu.get_barrier_semaphore()
    for step in range(1, count):
        pl.semaphore_signal(
            barrier, inc=1, device_id={"tok": lax.rem(me + step, count)}, device_id_type=MESH
        )
    pl.semaphore_signal(barrier, inc=1, device_id={"branch": other}, device_id_type=MESH)
    for peer in (below, above):
        pl.semaphore_signal(
            barrier, inc=1, device_id={"tok": peer, "branch": other}, device_id_type=MESH
        )

    loads = [
        pltpu.make_async_copy(q_hbm, qs, local_sem.at[0]),
        pltpu.make_async_copy(k_hbm, ks, local_sem.at[1]),
        pltpu.make_async_copy(v_hbm, vs, local_sem.at[2]),
        pltpu.make_async_copy(lat_hbm, lat, local_sem.at[3]),
        pltpu.make_async_copy(q_hbm.at[:, span(me)], rq.at[own_rows(me), :], local_sem.at[4]),
        pltpu.make_async_copy(k_hbm.at[:, span(me)], rk.at[own_rows(me), :], local_sem.at[5]),
        pltpu.make_async_copy(v_hbm.at[:, span(me)], rv.at[own_rows(me), :], local_sem.at[6]),
        pltpu.make_async_copy(kt_hbm.at[:, :, span(me)], kt, local_sem.at[7]),
        pltpu.make_async_copy(mt_hbm.at[:, :, span(me)], mt, local_sem.at[8]),
        pltpu.make_async_copy(ow_hbm.at[:, span(me)], ow, local_sem.at[9]),
        pltpu.make_async_copy(ci_hbm, ci, local_sem.at[10]),
        pltpu.make_async_copy(gain_hbm, gain, local_sem.at[11]),
        pltpu.make_async_copy(co_hbm, co, local_sem.at[12]),
    ]
    for load in loads:
        load.start()
    for load in loads[:4]:
        load.wait()
    late[1] = jnp.concatenate([lat[:half, :], lat[half:, :]], axis=1)

    pl.semaphore_wait(barrier, count + 2)

    sends = []
    for which, (source, target) in enumerate(((qs, rq), (ks, rk), (vs, rv))):
        for step in range(1, count):
            peer = lax.rem(me + step, count)
            copy = pltpu.make_async_remote_copy(
                src_ref=source.at[:, span(peer)],
                dst_ref=target.at[own_rows(me), :],
                send_sem=send_sem.at[which, step],
                recv_sem=recv_sem.at[which, me],
                device_id={"tok": peer},
                device_id_type=MESH,
            )
            copy.start()
            sends.append(copy)

    def latent_copy(peer, slot):
        return pltpu.make_async_remote_copy(
            src_ref=late.at[1],
            dst_ref=late.at[slot],
            send_sem=lat_send.at[slot],
            recv_sem=lat_recv.at[slot],
            device_id={"tok": peer},
            device_id_type=MESH,
        )

    @pl.when(has_low)
    def _():
        latent_copy(below, 2).start()

    @pl.when(has_high)
    def _():
        latent_copy(above, 0).start()

    def arrived(which, target):
        for step in range(1, count):
            peer = lax.rem(me + step, count)
            pltpu.make_async_remote_copy(
                src_ref=target.at[own_rows(peer), :],
                dst_ref=target.at[own_rows(peer), :],
                send_sem=send_sem.at[which, step],
                recv_sem=recv_sem.at[which, peer],
                device_id={"tok": peer},
                device_id_type=MESH,
            ).wait_recv()

    for load in loads[4:]:
        load.wait()
    for frame in range(count):
        key_rows = kt[kb_s[frame]].astype(jnp.float32)
        mouse_rows = mt[ms_s[frame]].astype(jnp.float32)
        for which, term in enumerate((key_rows + mouse_rows, mouse_rows, key_rows)):
            for part in range(2):
                act[part, which, frame : frame + 1, :] = term[part : part + 1, :]
    for which in range(3):
        spread = jnp.broadcast_to(act[0, which][:, None, :], (count, rows, cols))
        kbias[which] = spread.reshape(tokens, cols).astype(jnp.bfloat16)
    wbig[...] = jnp.zeros_like(wbig)
    for place in range(2):
        for shift in range(2):
            out_at = (place * 2 + shift) * dec
            for first in range(3):
                for second in range(3):
                    line, column = place + first, shift + second
                    second_half = column in (0, 3)
                    part = {0: 1, 1: 0, 2: 1, 3: 0}[column]
                    at = second_half * 2 * patch + line * 2 * lat_ch + part * lat_ch
                    from_at = (first * 3 + second) * lat_ch
                    wbig[at : at + lat_ch, out_at : out_at + dec] = ci[
                        from_at : from_at + lat_ch, :
                    ]
    colour_count = co.shape[1]
    spare = jnp.zeros((8 - colour_count, dec), jnp.float32)
    padded = [part for at in range(9) for part in (co[at].astype(jnp.float32), spare)]
    vt[...] = jnp.concatenate(padded, axis=0).astype(jnp.bfloat16)
    from_lane = lax.broadcasted_iota(jnp.int32, weave.shape, 0)
    to_lane = lax.broadcasted_iota(jnp.int32, weave.shape, 1)
    from_at = lax.rem(from_lane, 4 * rows)
    woven = 2 * from_at + from_lane // (4 * rows)
    weave[...] = jnp.where((woven == to_lane) & (from_at < 2 * rows), 1.0, 0.0).astype(
        jnp.bfloat16
    )

    arrived(0, rq)
    arrived(1, rk)
    factor = HEAD_DIM ** (-0.5) * math.log2(math.e)
    totals = []
    for head in range(heads):
        lanes = slice(head * HEAD_DIM, (head + 1) * HEAD_DIM)
        query = rq[:, lanes]
        key = rk[:, lanes]
        both = jnp.concatenate([query, query], axis=1)
        for which in range(4):
            if which < 3:
                scores = contract_last(
                    both, jnp.concatenate([key, kbias[which, :, lanes]], axis=1)
                )
            else:
                scores = contract_last(query, key)
            top = jnp.max(scores, axis=1, keepdims=True)
            raised = jnp.exp2((scores - top) * factor)
            totals.append(jnp.sum(raised, axis=1, keepdims=True))
            wts[head * 4 + which] = raised.astype(jnp.bfloat16)
    arrived(2, rv)
    combined = []
    for head in range(heads):
        lanes = slice(head * HEAD_DIM, (head + 1) * HEAD_DIM)
        plain = rv[:, lanes].astype(jnp.float32).reshape(count, rows, HEAD_DIM)
        mixed = None
        for which in range(4):
            if which < 3:
                value = plain + act[1, which, :, lanes][:, None, :]
                value = value.reshape(tokens, HEAD_DIM).astype(jnp.bfloat16)
            else:
                value = rv[:, lanes]
            summed = jnp.dot(wts[head * 4 + which], value, preferred_element_type=jnp.float32)
            attended = (summed / totals[head * 4 + which]).astype(jnp.bfloat16)
            term = guide_s[which] * attended.astype(jnp.float32)
            mixed = term if mixed is None else mixed + term
        combined.append(mixed.astype(jnp.bfloat16))
    joined = jnp.concatenate(combined, axis=1).reshape(count, 2, half, cols)
    blank = jnp.zeros(ow.shape, ow.dtype)
    left_weight = jnp.concatenate([ow[...], blank], axis=0)
    right_weight = jnp.concatenate([blank, ow[...]], axis=0)
    part_sums = contract_last(
        joined[:, 0].reshape(count * half, cols), left_weight
    ) + contract_last(joined[:, 1].reshape(count * half, cols), right_weight)
    psend[...] = part_sums.reshape(count, half, 2 * patch).astype(psend.dtype)

    for step in range(1, count):
        peer = lax.rem(me + step, count)
        copy = pltpu.make_async_remote_copy(
            src_ref=psend.at[peer],
            dst_ref=precv.at[me],
            send_sem=send2.at[step],
            recv_sem=recv2.at[me],
            device_id={"tok": peer},
            device_id_type=MESH,
        )
        copy.start()
        sends.append(copy)
    precv[me] = psend[me]
    for step in range(1, count):
        peer = lax.rem(me + step, count)
        pltpu.make_async_remote_copy(
            src_ref=psend.at[peer],
            dst_ref=precv.at[peer],
            send_sem=send2.at[step],
            recv_sem=recv2.at[peer],
            device_id={"tok": peer},
            device_id_type=MESH,
        ).wait_recv()
    ext[1, core] = jnp.sum(precv[...].astype(jnp.float32), axis=0)

    def exchange(at, slot, where):
        return pltpu.make_async_remote_copy(
            src_ref=ext.at[1, core],
            dst_ref=ext.at[slot, core],
            send_sem=x_send.at[at],
            recv_sem=x_recv.at[slot, core],
            device_id=where,
            device_id_type=MESH,
        )

    def expect(slot, branch):
        pltpu.make_async_remote_copy(
            src_ref=ext.at[1, core],
            dst_ref=ext.at[slot, branch],
            send_sem=x_send.at[0],
            recv_sem=x_recv.at[slot, branch],
            device_id={"branch": other},
            device_id_type=MESH,
        ).wait_recv()

    low_copies = [
        exchange(1, 2, {"tok": below, "branch": core}),
        exchange(2, 2, {"tok": below, "branch": other}),
    ]
    high_copies = [
        exchange(3, 0, {"tok": above, "branch": core}),
        exchange(4, 0, {"tok": above, "branch": other}),
    ]
    across = exchange(0, 1, {"branch": other})

    @pl.when(has_low)
    def _():
        for copy in low_copies:
            copy.start()

    @pl.when(has_high)
    def _():
        for copy in high_copies:
            copy.start()

    across.start()
    expect(1, other)

    @pl.when(has_low)
    def _():
        latent_copy(below, 0).wait_recv()
        expect(0, 0)
        expect(0, 1)

    @pl.when(has_high)
    def _():
        latent_copy(above, 2).wait_recv()
        expect(2, 0)
        expect(2, 1)

    velocity = ext[:, 0] + ext[:, 1]
    vel_out[:half, :] = velocity[1][:, :patch]
    vel_out[half:, :] = velocity[1][:, patch:]
    stepped = late[...] - step_size * velocity
    stepped = stepped.astype(jnp.bfloat16).astype(jnp.float32)
    lane = lax.broadcasted_iota(jnp.int32, (half, 2 * patch), 1)
    row = lax.broadcasted_iota(jnp.int32, (rows, 2 * patch), 0)
    wide = lax.broadcasted_iota(jnp.int32, (rows, 2 * patch), 1)
    blocks = []
    for low in range(2):
        one, two = stepped[low], stepped[low + 1]
        pair = jnp.concatenate(
            [
                jnp.where(lane < patch, one, pltpu.roll(two, patch, 1)),
                jnp.where(lane < patch, pltpu.roll(one, patch, 1), two),
            ],
            axis=0,
        )
        before = jnp.where(row == 0, 0.0, pltpu.roll(pair, 1, 0))
        after = jnp.where(row == rows - 1, 0.0, pltpu.roll(pair, rows - 1, 0))
        sides = jnp.where(lax.rem(wide, 2 * lat_ch) < lat_ch, after, before)
        blocks.append(jnp.concatenate([pair, sides], axis=1))
    windows = jnp.concatenate(blocks, axis=0).astype(jnp.bfloat16)
    gained = gain[...].reshape(1, dec)
    taps = []
    for shift in range(2):
        lines = []
        for place in range(2):
            out_at = (place * 2 + shift) * dec
            features = jnp.dot(
                windows, wbig[:, out_at : out_at + dec], preferred_element_type=jnp.float32
            )
            square = jnp.mean(features * features, axis=1, keepdims=True)
            scaled = features * lax.rsqrt(square + norm_eps) * gained
            lines.append(scaled / (1.0 + jnp.exp(-scaled)))
        ordered = jnp.concatenate(
            [
                jnp.where(has_low, lines[0][:rows], 0.0),
                lines[1][:rows],
                lines[0][rows:],
                jnp.where(has_high, lines[1][rows:], 0.0),
            ],
            axis=0,
        ).astype(jnp.bfloat16)
        taps.append(contract_last(vt[...], ordered))
    inner = lax.rem(lax.broadcasted_iota(jnp.int32, (8, 4 * rows), 1), rows)

    def tap(shift, first, second):
        at = (first * 3 + second) * 8
        return taps[shift][at : at + 8, :]

    halves = []
    for shift in range(2):
        out = None
        for first in range(3):
            if shift == 0:
                edge = jnp.where(inner == 0, 0.0, pltpu.roll(tap(1, first, 0), 1, 1))
                line = tap(0, first, 1) + tap(1, first, 2) + edge
            else:
                edge = jnp.where(
                    inner == rows - 1, 0.0, pltpu.roll(tap(0, first, 2), 4 * rows - 1, 1)
                )
                line = tap(0, first, 0) + tap(1, first, 1) + edge
            if first > 0:
                line = pltpu.roll(line, (4 - first) * rows, 1)
            out = line if out is None else out + line
        halves.append(out)
    rest = jnp.concatenate(halves, axis=1)
    parts = []
    for _ in range(3):
        parts.append(rest.astype(jnp.bfloat16).astype(jnp.float32))
        rest = rest - parts[-1]
    moved = jnp.dot(
        jnp.concatenate(parts, axis=0).astype(jnp.bfloat16),
        weave[...],
        preferred_element_type=jnp.float32,
    )
    colours = moved[:8] + moved[8:16] + moved[16:]
    for line in range(2):
        rgb_out[:, line, :] = colours[:colour_count, line * 2 * rows : (line + 1) * 2 * rows]

    for copy in sends:
        copy.wait_send()
    across.wait_send()

    @pl.when(has_low)
    def _():
        latent_copy(below, 2).wait_send()
        for copy in low_copies:
            copy.wait_send()

    @pl.when(has_high)
    def _():
        latent_copy(above, 0).wait_send()
        for copy in high_copies:
            copy.wait_send()


def fused_shards(
    queries,
    keys,
    values,
    keyboard,
    mouse,
    key_table,
    mouse_table,
    guidance,
    out_weight,
    latent,
    conv_in,
    gain,
    conv_out,
):
    count = lax.axis_size("tok")
    rows, width = queries.shape
    cols = width // (2 * count)
    tokens = rows * count
    patch = latent.shape[1]
    lat_ch, dec = conv_in.shape[2:]
    colours = conv_out.shape[3]
    half = rows // 2
    bf16, f32 = jnp.bfloat16, jnp.float32
    smem = pl.BlockSpec(memory_space=pltpu.SMEM)
    anywhere = pl.BlockSpec(memory_space=pl.ANY)
    vmem = pl.BlockSpec(memory_space=pltpu.VMEM)
    dma = pltpu.SemaphoreType.DMA
    velocity, rgb = pl.pallas_call(
        functools.partial(fused, count),
        out_shape=(
            jax.ShapeDtypeStruct((rows, patch), f32),
            jax.ShapeDtypeStruct((colours, 2, 2 * rows), f32),
        ),
        in_specs=[smem] * 3 + [anywhere] * 10,
        out_specs=(vmem, vmem),
        scratch_shapes=[
            pltpu.VMEM((rows, width), bf16),
            pltpu.VMEM((rows, width), bf16),
            pltpu.VMEM((rows, width), bf16),
            pltpu.VMEM((tokens, cols), bf16),
            pltpu.VMEM((tokens, cols), bf16),
            pltpu.VMEM((tokens, cols), bf16),
            pltpu.VMEM((key_table.shape[0], 2, cols), bf16),
            pltpu.VMEM((mouse_table.shape[0], 2, cols), bf16),
            pltpu.VMEM((patch, cols), bf16),
            pltpu.VMEM((rows, patch), f32),
            pltpu.VMEM((9 * lat_ch, dec), bf16),
            pltpu.VMEM((dec,), f32),
            pltpu.VMEM((9, colours, dec), bf16),
            pltpu.VMEM((2, 3, count, cols), f32),
            pltpu.VMEM((3, tokens, cols), bf16),
            pltpu.VMEM((4 * cols // HEAD_DIM, tokens, tokens), bf16),
            pltpu.VMEM((count, half, 2 * patch), bf16),
            pltpu.VMEM((count, half, 2 * patch), bf16),
            pltpu.VMEM((3, 2, half, 2 * patch), f32),
            pltpu.VMEM((3, half, 2 * patch), f32),
            pltpu.VMEM((4 * patch, 4 * dec), bf16),
            pltpu.VMEM((72, dec), bf16),
            pltpu.VMEM((8 * rows, 4 * rows), bf16),
            dma((13,)),
            dma((3, count)),
            dma((3, count)),
            dma((count,)),
            dma((count,)),
            dma((3,)),
            dma((3,)),
            dma((5,)),
            dma((3, 2)),
        ],
        compiler_params=pltpu.CompilerParams(collective_id=0, has_side_effects=True),
    )(
        keyboard,
        mouse,
        guidance,
        queries,
        keys,
        values,
        key_table,
        mouse_table,
        out_weight.T,
        latent,
        conv_in.reshape(9 * lat_ch, dec),
        gain,
        conv_out.transpose(0, 1, 3, 2).reshape(9, colours, dec),
    )
    return velocity, rgb


def solution(mesh):
    placed = (
        P(("groups", "tok"), None),
        P(("groups", "tok"), None),
        P(("groups", "tok"), None),
        P("groups"),
        P("groups"),
        P(),
        P(),
        P(),
        P(),
        P(("groups", "tok"), None),
        P(),
        P(),
        P(),
    )

    def step(queries, keys, values, keyboard, *rest):
        count = lax.axis_size("tok")
        single = count == 8 and keyboard.shape[0] == count
        body = fused_shards if single else shards
        return body(queries, keys, values, keyboard, *rest)

    return jax.shard_map(
        step,
        mesh=mesh,
        in_specs=placed,
        out_specs=(P(("groups", "tok"), None), P(None, ("groups", "tok"), None)),
        check_vma=False,
    )
```

```python
import functools
import math

import jax
import jax.numpy as jnp
from jax import lax
from jax.experimental import pallas as pl
from jax.experimental.pallas import tpu as pltpu
from jax.sharding import PartitionSpec as P

MESH = pl.DeviceIdType.MESH

HEAD_DIM = 128


step_size = 0.25
norm_eps = 1e-06


def passed_along(value, axis, steps):
    count = lax.axis_size(axis)
    pairs = [(source, (source + steps) % count) for source in range(count)]
    return lax.ppermute(value, axis, pairs)


def with_halo(block, sides, width):
    for axis, dim in sides:
        count = lax.axis_size(axis)
        forward = [(i, i + 1) for i in range(count - 1)]
        backward = [(target, source) for source, target in forward]
        low = lax.ppermute(
            lax.slice_in_dim(block, block.shape[dim] - width, None, axis=dim), axis, forward
        )
        high = lax.ppermute(lax.slice_in_dim(block, 0, width, axis=dim), axis, backward)
        block = jnp.concatenate([low, block, high], axis=dim)
    return block


def action_terms(keyboard, mouse, key_table, mouse_table, branch):
    flag_key = jnp.where(branch % 2 == 0, 1.0, 0.0).astype(jnp.float32)
    flag_mouse = jnp.where(branch < 2, 1.0, 0.0).astype(jnp.float32)
    pick_key = (
        keyboard[:, None] == jnp.arange(key_table.shape[0], dtype=jnp.int32)[None, :]
    ).astype(jnp.bfloat16)
    pick_mouse = (
        mouse[:, None] == jnp.arange(mouse_table.shape[0], dtype=jnp.int32)[None, :]
    ).astype(jnp.bfloat16)
    rows_key = jnp.einsum("fk,kcd->fcd", pick_key, key_table, preferred_element_type=jnp.float32)
    rows_mouse = jnp.einsum(
        "fk,kcd->fcd", pick_mouse, mouse_table, preferred_element_type=jnp.float32
    )
    return flag_key * rows_key + flag_mouse * rows_mouse


def pick_heads(array, first, taken, sets):
    lead = array.shape[:-1]
    split = array.reshape(lead + (sets, -1, HEAD_DIM))
    kept = lax.dynamic_slice_in_dim(split, first, taken, len(lead) + 1)
    return kept.reshape(lead + (sets * taken * HEAD_DIM,))


def heads_layout(array, rounds, sets):
    rows, width = array.shape
    piece = rows // rounds
    grouped = array.reshape(rounds, piece, sets, width // sets)
    return grouped.transpose(0, 2, 1, 3).reshape(rows * sets, width // sets)


def tokens_layout(array, rounds, sets):
    rows, width = array.shape
    piece = rows // (rounds * sets)
    grouped = array.reshape(rounds, sets, piece, width)
    return grouped.transpose(0, 2, 1, 3).reshape(rounds * piece, sets * width)


def attend(local_q, local_k, local_v, key_bias, value_term, rounds, sets):
    rows, width = local_q.shape
    heads_here = width // HEAD_DIM
    count_branches = key_bias.shape[0]
    frames = key_bias.shape[1]
    block = rows // frames
    scale = HEAD_DIM ** (-0.5)
    query = local_q.reshape(rows, heads_here, HEAD_DIM)
    bias_heads = key_bias.reshape(count_branches, frames, heads_here, HEAD_DIM)
    frame_scores = jnp.einsum(
        "qhd,bfhd->bhqf", query, bias_heads, preferred_element_type=jnp.float32
    )

    def visit(block_keys, block_values, carry):
        top, total, summed = carry
        base = jnp.einsum(
            "qhd,khd->hqk",
            query,
            block_keys.reshape(rows, heads_here, HEAD_DIM),
            preferred_element_type=jnp.float32,
        )
        grouped = base.reshape(heads_here, rows, frames, block)
        plain_values = block_values.astype(jnp.float32).reshape(frames, block, width)
        tops, totals, sums = ([], [], [])
        for which in range(count_branches):
            scores = (grouped + frame_scores[which][..., None]).reshape(
                heads_here, rows, rows
            ) * scale
            fresh = jnp.maximum(top[which], jnp.max(scores, axis=-1))
            shrink = jnp.exp(top[which] - fresh)
            raised = jnp.exp(scores - fresh[..., None])
            shifted = (plain_values + value_term[which][:, None, :]).astype(jnp.bfloat16)
            shifted = shifted.reshape(rows, heads_here, HEAD_DIM)
            product = jnp.einsum(
                "hqk,khd->hqd",
                raised.astype(jnp.bfloat16),
                shifted,
                preferred_element_type=jnp.float32,
            )
            tops.append(fresh)
            totals.append(total[which] * shrink + jnp.sum(raised, axis=-1))
            sums.append(summed[which] * shrink[..., None] + product)
        return (jnp.stack(tops), jnp.stack(totals), jnp.stack(sums))

    start = (
        jnp.full((count_branches, heads_here, rows), -jnp.inf, jnp.float32),
        jnp.zeros((count_branches, heads_here, rows), jnp.float32),
        jnp.zeros((count_branches, heads_here, rows, HEAD_DIM), jnp.float32),
    )
    carry = visit(local_k, local_v, start)

    def turn(step, state):
        block_keys, block_values, inner = state
        block_keys, block_values = passed_along((block_keys, block_values), "tok", sets)
        return (block_keys, block_values, visit(block_keys, block_values, inner))

    _, _, carry = lax.fori_loop(0, rounds - 1, turn, (local_k, local_v, carry))
    _, total, summed = carry
    attended = (summed / total[..., None]).astype(jnp.bfloat16)
    return attended.transpose(0, 2, 1, 3).reshape(count_branches, rows, heads_here * HEAD_DIM)


def clear_rows(array, depth, top_edge, bottom_edge):
    height = array.shape[0]
    place = jnp.arange(height, dtype=jnp.int32)
    drop = (place < depth) & top_edge | (place >= height - depth) & bottom_edge
    return jnp.where(drop[:, None, None], jnp.zeros_like(array), array)


def convolve(array, weight):
    rows = array.shape[0] - 2
    cols = array.shape[1]
    padded = jnp.pad(array, ((0, 0), (1, 1), (0, 0)))
    total = jnp.zeros((rows, cols, weight.shape[-1]), jnp.float32)
    for first in range(3):
        for second in range(3):
            window = padded[first : first + rows, second : second + cols, :]
            total = total + jnp.einsum(
                "rci,io->rco", window, weight[first, second], preferred_element_type=jnp.float32
            )
    return total


def normalize(features, gain):
    scaled = (
        features
        * lax.rsqrt(jnp.mean(features * features, axis=-1, keepdims=True) + norm_eps)
        * gain
    )
    return jax.nn.silu(scaled).astype(jnp.bfloat16)


def shards(
    queries,
    keys,
    values,
    keyboard,
    mouse,
    key_table,
    mouse_table,
    guidance,
    out_weight,
    latent,
    conv_in,
    gain,
    conv_out,
):
    count = lax.axis_size("tok")
    index = lax.axis_index("tok")
    branch = lax.axis_index("branch")
    sets = 8
    rounds = count // sets
    group = index % sets
    tok_dev, width = queries.shape
    per_group = width // (sets * HEAD_DIM)
    taken = per_group // 2
    first = branch * taken
    branches = [0, 1, 2, 3]
    spread_q = heads_layout(pick_heads(queries, first, taken, sets), rounds, sets)
    spread_k = heads_layout(pick_heads(keys, first, taken, sets), rounds, sets)
    spread_v = heads_layout(pick_heads(values, first, taken, sets), rounds, sets)
    local_q, local_k, local_v = (
        lax.all_to_all(spread_q, "tok", split_axis=0, concat_axis=0, tiled=True),
        lax.all_to_all(spread_k, "tok", split_axis=0, concat_axis=0, tiled=True),
        lax.all_to_all(spread_v, "tok", split_axis=0, concat_axis=0, tiled=True),
    )
    terms = jnp.stack(
        [action_terms(keyboard, mouse, key_table, mouse_table, which) for which in branches]
    )
    mine = pick_heads(terms, first, taken, sets)
    mine = mine.reshape(mine.shape[:-1] + (sets, -1))
    mine = lax.dynamic_index_in_dim(mine, group, 3, keepdims=False)
    key_bias = mine[:, :, 0].astype(jnp.bfloat16)
    value_term = mine[:, :, 1]
    outputs = attend(local_q, local_k, local_v, key_bias, value_term, rounds, sets)
    factors = [guidance[which] for which in branches]
    partial_value = factors[0] * outputs[0].astype(jnp.float32)
    for which in range(1, len(branches)):
        partial_value = partial_value + factors[which] * outputs[which].astype(jnp.float32)
    returned = lax.all_to_all(
        partial_value.astype(jnp.bfloat16), "tok", split_axis=0, concat_axis=0, tiled=True
    )
    split_weight = out_weight.reshape(sets, per_group, HEAD_DIM, -1)
    rows_weight = lax.dynamic_slice_in_dim(split_weight, first, taken, 1).reshape(
        sets * taken * HEAD_DIM, -1
    )
    projected = jnp.dot(
        tokens_layout(returned, rounds, sets), rows_weight, preferred_element_type=jnp.float32
    )
    velocity = lax.psum(projected, "branch")
    stepped = latent - step_size * velocity
    grid = (
        stepped.reshape(tok_dev, 2, 2, -1)
        .transpose(1, 0, 2, 3)
        .reshape(2, 2 * tok_dev, -1)
        .astype(jnp.bfloat16)
    )
    top_edge = index == 0
    bottom_edge = index == count - 1
    bordered = with_halo(grid, (("tok", 0),), 1)
    bordered = clear_rows(bordered, 1, top_edge, bottom_edge)
    hidden = normalize(convolve(bordered, conv_in), gain)
    hidden = with_halo(hidden, (("tok", 0),), 1)
    hidden = clear_rows(hidden, 1, top_edge, bottom_edge)
    colours = convolve(hidden, conv_out)
    return (velocity, colours.transpose(2, 0, 1))


def contract_last(left, right):
    return lax.dot_general(
        left, right, (((1,), (1,)), ((), ())), preferred_element_type=jnp.float32
    )


def fused(
    count,
    kb_hbm, ms_hbm, guide_hbm,
    q_hbm, k_hbm, v_hbm, kt_hbm, mt_hbm, ow_hbm, lat_hbm, ci_hbm, gain_hbm, co_hbm,
    vel_out, rgb_out,
    kb_s, ms_s, guide_s, qs, ks, vs, rq, rk, rv, kt, mt, ow, lat, ci, gain, co,
    act, kbias, wts, psend, precv, ext, late, wbig, vt, weave,
    local_sem, send_sem, recv_sem, send2, recv2, lat_send, lat_recv, x_send, x_recv, relay,
):
    me = lax.axis_index("tok")
    core = lax.axis_index("branch")
    other = 1 - core
    rows = q_hbm.shape[0]
    half = rows // 2
    cols = rq.shape[1]
    heads = cols // HEAD_DIM
    tokens = rows * count
    patch = lat_hbm.shape[1]
    dec = gain.shape[0]
    lat_ch = ci.shape[0] // 9
    below = lax.rem(me + count - 1, count)
    above = lax.rem(me + 1, count)
    has_low = me > 0
    has_high = me < count - 1

    plane, side = lax.div(me, 2), lax.rem(me, 2)
    beside = plane + 1 - 2 * lax.rem(plane, 2)
    opposite = plane + 2 - 4 * lax.div(plane, 2)
    mirror = 3 - plane
    middle = (plane == 1) | (plane == 2)
    near = [
        2 * opposite + side,
        2 * beside + 1 - side,
        2 * beside + side,
        2 * plane + 1 - side,
    ]
    facing = [2 * mirror + side, 2 * mirror + 1 - side]
    distant = 2 * opposite + 1 - side
    peers = facing + [distant] + near

    def span(index):
        return pl.ds(pl.multiple_of((2 * index + core) * cols, cols), cols)

    def own_rows(index):
        return pl.ds(pl.multiple_of(index * rows, rows), rows)

    ext[...] = jnp.zeros_like(ext)
    late[0] = jnp.zeros(late.shape[1:], late.dtype)
    late[2] = jnp.zeros(late.shape[1:], late.dtype)
    barrier = pltpu.get_barrier_semaphore()
    for peer in near:
        pl.semaphore_signal(barrier, inc=1, device_id={"tok": peer}, device_id_type=MESH)
    pl.semaphore_signal(barrier, inc=1, device_id={"branch": other}, device_id_type=MESH)

    @pl.when(middle)
    def _():
        for peer in facing:
            pl.semaphore_signal(barrier, inc=1, device_id={"tok": peer}, device_id_type=MESH)

    for exists, peer in ((has_low, below), (has_high, above)):

        @pl.when(exists)
        def _(peer=peer):
            pl.semaphore_signal(
                barrier, inc=1, device_id={"tok": peer, "branch": other}, device_id_type=MESH
            )

    loads = [
        pltpu.make_async_copy(q_hbm, qs, local_sem.at[0]),
        pltpu.make_async_copy(k_hbm, ks, local_sem.at[1]),
        pltpu.make_async_copy(v_hbm, vs, local_sem.at[2]),
        pltpu.make_async_copy(lat_hbm, lat, local_sem.at[3]),
        pltpu.make_async_copy(q_hbm.at[:, span(me)], rq.at[own_rows(me), :], local_sem.at[4]),
        pltpu.make_async_copy(k_hbm.at[:, span(me)], rk.at[own_rows(me), :], local_sem.at[5]),
        pltpu.make_async_copy(v_hbm.at[:, span(me)], rv.at[own_rows(me), :], local_sem.at[6]),
        pltpu.make_async_copy(kt_hbm.at[:, :, span(me)], kt, local_sem.at[7]),
        pltpu.make_async_copy(mt_hbm.at[:, :, span(me)], mt, local_sem.at[8]),
        pltpu.make_async_copy(ow_hbm.at[:, span(me)], ow, local_sem.at[9]),
        pltpu.make_async_copy(ci_hbm, ci, local_sem.at[10]),
        pltpu.make_async_copy(gain_hbm, gain, local_sem.at[11]),
        pltpu.make_async_copy(co_hbm, co, local_sem.at[12]),
        pltpu.make_async_copy(kb_hbm, kb_s, local_sem.at[13]),
        pltpu.make_async_copy(ms_hbm, ms_s, local_sem.at[14]),
        pltpu.make_async_copy(guide_hbm, guide_s, local_sem.at[15]),
    ]
    for load in loads:
        load.start()
    for load in loads[:4]:
        load.wait()
    late[1] = jnp.concatenate([lat[:half, :], lat[half:, :]], axis=1)

    def flag(condition):
        return jnp.where(condition, 1, 0)

    pl.semaphore_wait(barrier, 5 + 2 * flag(middle) + flag(has_low) + flag(has_high))
    pl.semaphore_signal(relay, inc=1, device_id={"tok": near[0]}, device_id_type=MESH)

    moves = ((qs, rq), (ks, rk), (vs, rv))

    def block_copy(which, at):
        source, target = moves[which]
        return pltpu.make_async_remote_copy(
            src_ref=source.at[:, span(peers[at])],
            dst_ref=target.at[own_rows(me), :],
            send_sem=send_sem.at[which, at],
            recv_sem=recv_sem.at[which, me],
            device_id={"tok": peers[at]},
            device_id_type=MESH,
        )

    @pl.when(middle)
    def _():
        for which in range(2):
            for at in range(2):
                block_copy(which, at).start()

    for which in range(2):
        for at in range(3, count - 1):
            block_copy(which, at).start()

    def latent_copy(peer, slot):
        return pltpu.make_async_remote_copy(
            src_ref=late.at[1],
            dst_ref=late.at[slot],
            send_sem=lat_send.at[slot],
            recv_sem=lat_recv.at[slot],
            device_id={"tok": peer},
            device_id_type=MESH,
        )

    @pl.when(has_low)
    def _():
        latent_copy(below, 2).start()

    @pl.when(has_high)
    def _():
        latent_copy(above, 0).start()

    pl.semaphore_wait(relay, 1)

    @pl.when(jnp.logical_not(middle))
    def _():
        for which in range(2):
            for at in range(2):
                block_copy(which, at).start()

    for which in range(2):
        block_copy(which, 2).start()
    for at in range(count - 1):
        block_copy(2, at).start()
    sends = [block_copy(which, at) for which in range(3) for at in range(count - 1)]

    def arrived(which, target):
        for step, peer in enumerate(peers):
            pltpu.make_async_remote_copy(
                src_ref=target.at[own_rows(peer), :],
                dst_ref=target.at[own_rows(peer), :],
                send_sem=send_sem.at[which, step],
                recv_sem=recv_sem.at[which, peer],
                device_id={"tok": peer},
                device_id_type=MESH,
            ).wait_recv()

    for load in loads[4:]:
        load.wait()
    for frame in range(count):
        key_rows = kt[kb_s[frame]].astype(jnp.float32)
        mouse_rows = mt[ms_s[frame]].astype(jnp.float32)
        for which, term in enumerate((key_rows + mouse_rows, mouse_rows, key_rows)):
            for part in range(2):
                act[part, which, frame : frame + 1, :] = term[part : part + 1, :]
    for which in range(3):
        spread = jnp.broadcast_to(act[0, which][:, None, :], (count, rows, cols))
        kbias[which] = spread.reshape(tokens, cols).astype(jnp.bfloat16)
    wbig[...] = jnp.zeros_like(wbig)
    for place in range(2):
        for shift in range(2):
            out_at = (place * 2 + shift) * dec
            for first in range(3):
                for second in range(3):
                    line, column = place + first, shift + second
                    second_half = column in (0, 3)
                    part = {0: 1, 1: 0, 2: 1, 3: 0}[column]
                    at = second_half * 2 * patch + line * 2 * lat_ch + part * lat_ch
                    from_at = (first * 3 + second) * lat_ch
                    wbig[at : at + lat_ch, out_at : out_at + dec] = ci[
                        from_at : from_at + lat_ch, :
                    ]
    colour_count = co.shape[1]
    spare = jnp.zeros((8 - colour_count, dec), jnp.float32)
    padded = [part for at in range(9) for part in (co[at].astype(jnp.float32), spare)]
    vt[...] = jnp.concatenate(padded, axis=0).astype(jnp.bfloat16)
    from_lane = lax.broadcasted_iota(jnp.int32, weave.shape, 0)
    to_lane = lax.broadcasted_iota(jnp.int32, weave.shape, 1)
    from_at = lax.rem(from_lane, 4 * rows)
    woven = 2 * from_at + from_lane // (4 * rows)
    weave[...] = jnp.where((woven == to_lane) & (from_at < 2 * rows), 1.0, 0.0).astype(
        jnp.bfloat16
    )

    arrived(0, rq)
    arrived(1, rk)
    factor = HEAD_DIM ** (-0.5) * math.log2(math.e)
    totals = []
    for head in range(heads):
        lanes = slice(head * HEAD_DIM, (head + 1) * HEAD_DIM)
        query = rq[:, lanes]
        key = rk[:, lanes]
        both = jnp.concatenate([query, query], axis=1)
        for which in range(4):
            if which < 3:
                scores = contract_last(
                    both, jnp.concatenate([key, kbias[which, :, lanes]], axis=1)
                )
            else:
                scores = contract_last(query, key)
            top = jnp.max(scores, axis=1, keepdims=True)
            raised = jnp.exp2((scores - top) * factor)
            totals.append(jnp.sum(raised, axis=1, keepdims=True))
            wts[head * 4 + which] = raised.astype(jnp.bfloat16)
    arrived(2, rv)
    combined = []
    for head in range(heads):
        lanes = slice(head * HEAD_DIM, (head + 1) * HEAD_DIM)
        plain = rv[:, lanes].astype(jnp.float32).reshape(count, rows, HEAD_DIM)
        mixed = None
        for which in range(4):
            if which < 3:
                value = plain + act[1, which, :, lanes][:, None, :]
                value = value.reshape(tokens, HEAD_DIM).astype(jnp.bfloat16)
            else:
                value = rv[:, lanes]
            summed = jnp.dot(wts[head * 4 + which], value, preferred_element_type=jnp.float32)
            attended = (summed / totals[head * 4 + which]).astype(jnp.bfloat16)
            term = guide_s[which] * attended.astype(jnp.float32)
            mixed = term if mixed is None else mixed + term
        combined.append(mixed.astype(jnp.bfloat16))
    joined = jnp.concatenate(combined, axis=1).reshape(count, 2, half, cols)
    blank = jnp.zeros(ow.shape, ow.dtype)
    left_weight = jnp.concatenate([ow[...], blank], axis=0)
    right_weight = jnp.concatenate([blank, ow[...]], axis=0)
    part_sums = contract_last(
        joined[:, 0].reshape(count * half, cols), left_weight
    ) + contract_last(joined[:, 1].reshape(count * half, cols), right_weight)
    psend[...] = part_sums.reshape(count, half, 2 * patch).astype(psend.dtype)

    for step, peer in enumerate(peers):
        copy = pltpu.make_async_remote_copy(
            src_ref=psend.at[peer],
            dst_ref=precv.at[me],
            send_sem=send2.at[step],
            recv_sem=recv2.at[me],
            device_id={"tok": peer},
            device_id_type=MESH,
        )
        copy.start()
        sends.append(copy)
    precv[me] = psend[me]
    for step, peer in enumerate(peers):
        pltpu.make_async_remote_copy(
            src_ref=psend.at[peer],
            dst_ref=precv.at[peer],
            send_sem=send2.at[step],
            recv_sem=recv2.at[peer],
            device_id={"tok": peer},
            device_id_type=MESH,
        ).wait_recv()
    ext[1, core] = jnp.sum(precv[...].astype(jnp.float32), axis=0)

    def exchange(at, slot, where):
        return pltpu.make_async_remote_copy(
            src_ref=ext.at[1, core],
            dst_ref=ext.at[slot, core],
            send_sem=x_send.at[at],
            recv_sem=x_recv.at[slot, core],
            device_id=where,
            device_id_type=MESH,
        )

    def expect(slot, branch):
        pltpu.make_async_remote_copy(
            src_ref=ext.at[1, core],
            dst_ref=ext.at[slot, branch],
            send_sem=x_send.at[0],
            recv_sem=x_recv.at[slot, branch],
            device_id={"branch": other},
            device_id_type=MESH,
        ).wait_recv()

    low_copies = [
        exchange(1, 2, {"tok": below, "branch": core}),
        exchange(2, 2, {"tok": below, "branch": other}),
    ]
    high_copies = [
        exchange(3, 0, {"tok": above, "branch": core}),
        exchange(4, 0, {"tok": above, "branch": other}),
    ]
    across = exchange(0, 1, {"branch": other})

    @pl.when(has_low)
    def _():
        for copy in low_copies:
            copy.start()

    @pl.when(has_high)
    def _():
        for copy in high_copies:
            copy.start()

    across.start()
    expect(1, other)

    @pl.when(has_low)
    def _():
        latent_copy(below, 0).wait_recv()
        expect(0, 0)
        expect(0, 1)

    @pl.when(has_high)
    def _():
        latent_copy(above, 2).wait_recv()
        expect(2, 0)
        expect(2, 1)

    velocity = ext[:, 0] + ext[:, 1]
    vel_out[:half, :] = velocity[1][:, :patch]
    vel_out[half:, :] = velocity[1][:, patch:]
    stepped = late[...] - step_size * velocity
    stepped = stepped.astype(jnp.bfloat16).astype(jnp.float32)
    lane = lax.broadcasted_iota(jnp.int32, (half, 2 * patch), 1)
    row = lax.broadcasted_iota(jnp.int32, (rows, 2 * patch), 0)
    wide = lax.broadcasted_iota(jnp.int32, (rows, 2 * patch), 1)
    blocks = []
    for low in range(2):
        one, two = stepped[low], stepped[low + 1]
        pair = jnp.concatenate(
            [
                jnp.where(lane < patch, one, pltpu.roll(two, patch, 1)),
                jnp.where(lane < patch, pltpu.roll(one, patch, 1), two),
            ],
            axis=0,
        )
        before = jnp.where(row == 0, 0.0, pltpu.roll(pair, 1, 0))
        after = jnp.where(row == rows - 1, 0.0, pltpu.roll(pair, rows - 1, 0))
        sides = jnp.where(lax.rem(wide, 2 * lat_ch) < lat_ch, after, before)
        blocks.append(jnp.concatenate([pair, sides], axis=1))
    windows = jnp.concatenate(blocks, axis=0).astype(jnp.bfloat16)
    gained = gain[...].reshape(1, dec)
    taps = []
    for shift in range(2):
        lines = []
        for place in range(2):
            out_at = (place * 2 + shift) * dec
            features = jnp.dot(
                windows, wbig[:, out_at : out_at + dec], preferred_element_type=jnp.float32
            )
            square = jnp.mean(features * features, axis=1, keepdims=True)
            scaled = features * lax.rsqrt(square + norm_eps) * gained
            lines.append(scaled / (1.0 + jnp.exp(-scaled)))
        ordered = jnp.concatenate(
            [
                jnp.where(has_low, lines[0][:rows], 0.0),
                lines[1][:rows],
                lines[0][rows:],
                jnp.where(has_high, lines[1][rows:], 0.0),
            ],
            axis=0,
        ).astype(jnp.bfloat16)
        taps.append(contract_last(vt[...], ordered))
    inner = lax.rem(lax.broadcasted_iota(jnp.int32, (8, 4 * rows), 1), rows)

    def tap(shift, first, second):
        at = (first * 3 + second) * 8
        return taps[shift][at : at + 8, :]

    halves = []
    for shift in range(2):
        out = None
        for first in range(3):
            if shift == 0:
                edge = jnp.where(inner == 0, 0.0, pltpu.roll(tap(1, first, 0), 1, 1))
                line = tap(0, first, 1) + tap(1, first, 2) + edge
            else:
                edge = jnp.where(
                    inner == rows - 1, 0.0, pltpu.roll(tap(0, first, 2), 4 * rows - 1, 1)
                )
                line = tap(0, first, 0) + tap(1, first, 1) + edge
            if first > 0:
                line = pltpu.roll(line, (4 - first) * rows, 1)
            out = line if out is None else out + line
        halves.append(out)
    rest = jnp.concatenate(halves, axis=1)
    parts = []
    for _ in range(3):
        parts.append(rest.astype(jnp.bfloat16).astype(jnp.float32))
        rest = rest - parts[-1]
    moved = jnp.dot(
        jnp.concatenate(parts, axis=0).astype(jnp.bfloat16),
        weave[...],
        preferred_element_type=jnp.float32,
    )
    colours = moved[:8] + moved[8:16] + moved[16:]
    for line in range(2):
        rgb_out[:, line, :] = colours[:colour_count, line * 2 * rows : (line + 1) * 2 * rows]

    for copy in sends:
        copy.wait_send()
    across.wait_send()

    @pl.when(has_low)
    def _():
        latent_copy(below, 2).wait_send()
        for copy in low_copies:
            copy.wait_send()

    @pl.when(has_high)
    def _():
        latent_copy(above, 0).wait_send()
        for copy in high_copies:
            copy.wait_send()


def fused_shards(
    queries,
    keys,
    values,
    keyboard,
    mouse,
    key_table,
    mouse_table,
    guidance,
    out_weight,
    latent,
    conv_in,
    gain,
    conv_out,
):
    count = lax.axis_size("tok")
    rows, width = queries.shape
    cols = width // (2 * count)
    tokens = rows * count
    patch = latent.shape[1]
    lat_ch, dec = conv_in.shape[2:]
    colours = conv_out.shape[3]
    half = rows // 2
    bf16, f32 = jnp.bfloat16, jnp.float32
    hbm = pl.BlockSpec(memory_space=pltpu.HBM)
    vmem = pl.BlockSpec(memory_space=pltpu.VMEM)
    dma = pltpu.SemaphoreType.DMA

    def pin(array):
        return pltpu.with_memory_space_constraint(array, pltpu.HBM)

    velocity, rgb = pl.pallas_call(
        functools.partial(fused, count),
        out_shape=(
            jax.ShapeDtypeStruct((rows, patch), f32),
            jax.ShapeDtypeStruct((colours, 2, 2 * rows), f32),
        ),
        in_specs=[hbm] * 13,
        out_specs=(vmem, vmem),
        scratch_shapes=[
            pltpu.SMEM(keyboard.shape, jnp.int32),
            pltpu.SMEM(mouse.shape, jnp.int32),
            pltpu.SMEM(guidance.shape, f32),
            pltpu.VMEM((rows, width), bf16),
            pltpu.VMEM((rows, width), bf16),
            pltpu.VMEM((rows, width), bf16),
            pltpu.VMEM((tokens, cols), bf16),
            pltpu.VMEM((tokens, cols), bf16),
            pltpu.VMEM((tokens, cols), bf16),
            pltpu.VMEM((key_table.shape[0], 2, cols), bf16),
            pltpu.VMEM((mouse_table.shape[0], 2, cols), bf16),
            pltpu.VMEM((patch, cols), bf16),
            pltpu.VMEM((rows, patch), f32),
            pltpu.VMEM((9 * lat_ch, dec), bf16),
            pltpu.VMEM((dec,), f32),
            pltpu.VMEM((9, colours, dec), bf16),
            pltpu.VMEM((2, 3, count, cols), f32),
            pltpu.VMEM((3, tokens, cols), bf16),
            pltpu.VMEM((4 * cols // HEAD_DIM, tokens, tokens), bf16),
            pltpu.VMEM((count, half, 2 * patch), bf16),
            pltpu.VMEM((count, half, 2 * patch), bf16),
            pltpu.VMEM((3, 2, half, 2 * patch), f32),
            pltpu.VMEM((3, half, 2 * patch), f32),
            pltpu.VMEM((4 * patch, 4 * dec), bf16),
            pltpu.VMEM((72, dec), bf16),
            pltpu.VMEM((8 * rows, 4 * rows), bf16),
            dma((16,)),
            dma((3, count)),
            dma((3, count)),
            dma((count,)),
            dma((count,)),
            dma((3,)),
            dma((3,)),
            dma((5,)),
            dma((3, 2)),
            pltpu.SemaphoreType.REGULAR,
        ],
        compiler_params=pltpu.CompilerParams(collective_id=0, has_side_effects=True, vmem_limit_bytes=16 * 2**20),
    )(
        pin(keyboard),
        pin(mouse),
        pin(guidance),
        pin(queries),
        pin(keys),
        pin(values),
        pin(key_table),
        pin(mouse_table),
        pin(out_weight.T),
        pin(latent),
        pin(conv_in.reshape(9 * lat_ch, dec)),
        pin(gain),
        pin(conv_out.transpose(0, 1, 3, 2).reshape(9, colours, dec)),
    )
    return velocity, rgb


def solution(mesh):
    placed = (
        P(("groups", "tok"), None),
        P(("groups", "tok"), None),
        P(("groups", "tok"), None),
        P("groups"),
        P("groups"),
        P(),
        P(),
        P(),
        P(),
        P(("groups", "tok"), None),
        P(),
        P(),
        P(),
    )

    def step(queries, keys, values, keyboard, *rest):
        count = lax.axis_size("tok")
        single = count == 8 and keyboard.shape[0] == count
        body = fused_shards if single else shards
        return body(queries, keys, values, keyboard, *rest)

    return jax.shard_map(
        step,
        mesh=mesh,
        in_specs=placed,
        out_specs=(P(("groups", "tok"), None), P(None, ("groups", "tok"), None)),
        check_vma=False,
    )
```

```python
import functools
import math

import jax
import jax.numpy as jnp
from jax import lax
from jax.experimental import pallas as pl
from jax.experimental.pallas import tpu as pltpu
from jax.sharding import PartitionSpec as P

MESH = pl.DeviceIdType.MESH

HEAD_DIM = 128


step_size = 0.25
norm_eps = 1e-06


def passed_along(value, axis, steps):
    count = lax.axis_size(axis)
    pairs = [(source, (source + steps) % count) for source in range(count)]
    return lax.ppermute(value, axis, pairs)


def with_halo(block, sides, width):
    for axis, dim in sides:
        count = lax.axis_size(axis)
        forward = [(i, i + 1) for i in range(count - 1)]
        backward = [(target, source) for source, target in forward]
        low = lax.ppermute(
            lax.slice_in_dim(block, block.shape[dim] - width, None, axis=dim), axis, forward
        )
        high = lax.ppermute(lax.slice_in_dim(block, 0, width, axis=dim), axis, backward)
        block = jnp.concatenate([low, block, high], axis=dim)
    return block


def action_terms(keyboard, mouse, key_table, mouse_table, branch):
    flag_key = jnp.where(branch % 2 == 0, 1.0, 0.0).astype(jnp.float32)
    flag_mouse = jnp.where(branch < 2, 1.0, 0.0).astype(jnp.float32)
    pick_key = (
        keyboard[:, None] == jnp.arange(key_table.shape[0], dtype=jnp.int32)[None, :]
    ).astype(jnp.bfloat16)
    pick_mouse = (
        mouse[:, None] == jnp.arange(mouse_table.shape[0], dtype=jnp.int32)[None, :]
    ).astype(jnp.bfloat16)
    rows_key = jnp.einsum("fk,kcd->fcd", pick_key, key_table, preferred_element_type=jnp.float32)
    rows_mouse = jnp.einsum(
        "fk,kcd->fcd", pick_mouse, mouse_table, preferred_element_type=jnp.float32
    )
    return flag_key * rows_key + flag_mouse * rows_mouse


def pick_heads(array, first, taken, sets):
    lead = array.shape[:-1]
    split = array.reshape(lead + (sets, -1, HEAD_DIM))
    kept = lax.dynamic_slice_in_dim(split, first, taken, len(lead) + 1)
    return kept.reshape(lead + (sets * taken * HEAD_DIM,))


def heads_layout(array, rounds, sets):
    rows, width = array.shape
    piece = rows // rounds
    grouped = array.reshape(rounds, piece, sets, width // sets)
    return grouped.transpose(0, 2, 1, 3).reshape(rows * sets, width // sets)


def tokens_layout(array, rounds, sets):
    rows, width = array.shape
    piece = rows // (rounds * sets)
    grouped = array.reshape(rounds, sets, piece, width)
    return grouped.transpose(0, 2, 1, 3).reshape(rounds * piece, sets * width)


def attend(local_q, local_k, local_v, key_bias, value_term, rounds, sets):
    rows, width = local_q.shape
    heads_here = width // HEAD_DIM
    count_branches = key_bias.shape[0]
    frames = key_bias.shape[1]
    block = rows // frames
    scale = HEAD_DIM ** (-0.5)
    query = local_q.reshape(rows, heads_here, HEAD_DIM)
    bias_heads = key_bias.reshape(count_branches, frames, heads_here, HEAD_DIM)
    frame_scores = jnp.einsum(
        "qhd,bfhd->bhqf", query, bias_heads, preferred_element_type=jnp.float32
    )

    def visit(block_keys, block_values, carry):
        top, total, summed = carry
        base = jnp.einsum(
            "qhd,khd->hqk",
            query,
            block_keys.reshape(rows, heads_here, HEAD_DIM),
            preferred_element_type=jnp.float32,
        )
        grouped = base.reshape(heads_here, rows, frames, block)
        plain_values = block_values.astype(jnp.float32).reshape(frames, block, width)
        tops, totals, sums = ([], [], [])
        for which in range(count_branches):
            scores = (grouped + frame_scores[which][..., None]).reshape(
                heads_here, rows, rows
            ) * scale
            fresh = jnp.maximum(top[which], jnp.max(scores, axis=-1))
            shrink = jnp.exp(top[which] - fresh)
            raised = jnp.exp(scores - fresh[..., None])
            shifted = (plain_values + value_term[which][:, None, :]).astype(jnp.bfloat16)
            shifted = shifted.reshape(rows, heads_here, HEAD_DIM)
            product = jnp.einsum(
                "hqk,khd->hqd",
                raised.astype(jnp.bfloat16),
                shifted,
                preferred_element_type=jnp.float32,
            )
            tops.append(fresh)
            totals.append(total[which] * shrink + jnp.sum(raised, axis=-1))
            sums.append(summed[which] * shrink[..., None] + product)
        return (jnp.stack(tops), jnp.stack(totals), jnp.stack(sums))

    start = (
        jnp.full((count_branches, heads_here, rows), -jnp.inf, jnp.float32),
        jnp.zeros((count_branches, heads_here, rows), jnp.float32),
        jnp.zeros((count_branches, heads_here, rows, HEAD_DIM), jnp.float32),
    )
    carry = visit(local_k, local_v, start)

    def turn(step, state):
        block_keys, block_values, inner = state
        block_keys, block_values = passed_along((block_keys, block_values), "tok", sets)
        return (block_keys, block_values, visit(block_keys, block_values, inner))

    _, _, carry = lax.fori_loop(0, rounds - 1, turn, (local_k, local_v, carry))
    _, total, summed = carry
    attended = (summed / total[..., None]).astype(jnp.bfloat16)
    return attended.transpose(0, 2, 1, 3).reshape(count_branches, rows, heads_here * HEAD_DIM)


def clear_rows(array, depth, top_edge, bottom_edge):
    height = array.shape[0]
    place = jnp.arange(height, dtype=jnp.int32)
    drop = (place < depth) & top_edge | (place >= height - depth) & bottom_edge
    return jnp.where(drop[:, None, None], jnp.zeros_like(array), array)


def convolve(array, weight):
    rows = array.shape[0] - 2
    cols = array.shape[1]
    padded = jnp.pad(array, ((0, 0), (1, 1), (0, 0)))
    total = jnp.zeros((rows, cols, weight.shape[-1]), jnp.float32)
    for first in range(3):
        for second in range(3):
            window = padded[first : first + rows, second : second + cols, :]
            total = total + jnp.einsum(
                "rci,io->rco", window, weight[first, second], preferred_element_type=jnp.float32
            )
    return total


def normalize(features, gain):
    scaled = (
        features
        * lax.rsqrt(jnp.mean(features * features, axis=-1, keepdims=True) + norm_eps)
        * gain
    )
    return jax.nn.silu(scaled).astype(jnp.bfloat16)


def shards(
    queries,
    keys,
    values,
    keyboard,
    mouse,
    key_table,
    mouse_table,
    guidance,
    out_weight,
    latent,
    conv_in,
    gain,
    conv_out,
):
    count = lax.axis_size("tok")
    index = lax.axis_index("tok")
    branch = lax.axis_index("branch")
    sets = 8
    rounds = count // sets
    group = index % sets
    tok_dev, width = queries.shape
    per_group = width // (sets * HEAD_DIM)
    taken = per_group // 2
    first = branch * taken
    branches = [0, 1, 2, 3]
    spread_q = heads_layout(pick_heads(queries, first, taken, sets), rounds, sets)
    spread_k = heads_layout(pick_heads(keys, first, taken, sets), rounds, sets)
    spread_v = heads_layout(pick_heads(values, first, taken, sets), rounds, sets)
    local_q, local_k, local_v = (
        lax.all_to_all(spread_q, "tok", split_axis=0, concat_axis=0, tiled=True),
        lax.all_to_all(spread_k, "tok", split_axis=0, concat_axis=0, tiled=True),
        lax.all_to_all(spread_v, "tok", split_axis=0, concat_axis=0, tiled=True),
    )
    terms = jnp.stack(
        [action_terms(keyboard, mouse, key_table, mouse_table, which) for which in branches]
    )
    mine = pick_heads(terms, first, taken, sets)
    mine = mine.reshape(mine.shape[:-1] + (sets, -1))
    mine = lax.dynamic_index_in_dim(mine, group, 3, keepdims=False)
    key_bias = mine[:, :, 0].astype(jnp.bfloat16)
    value_term = mine[:, :, 1]
    outputs = attend(local_q, local_k, local_v, key_bias, value_term, rounds, sets)
    factors = [guidance[which] for which in branches]
    partial_value = factors[0] * outputs[0].astype(jnp.float32)
    for which in range(1, len(branches)):
        partial_value = partial_value + factors[which] * outputs[which].astype(jnp.float32)
    returned = lax.all_to_all(
        partial_value.astype(jnp.bfloat16), "tok", split_axis=0, concat_axis=0, tiled=True
    )
    split_weight = out_weight.reshape(sets, per_group, HEAD_DIM, -1)
    rows_weight = lax.dynamic_slice_in_dim(split_weight, first, taken, 1).reshape(
        sets * taken * HEAD_DIM, -1
    )
    projected = jnp.dot(
        tokens_layout(returned, rounds, sets), rows_weight, preferred_element_type=jnp.float32
    )
    velocity = lax.psum(projected, "branch")
    stepped = latent - step_size * velocity
    grid = (
        stepped.reshape(tok_dev, 2, 2, -1)
        .transpose(1, 0, 2, 3)
        .reshape(2, 2 * tok_dev, -1)
        .astype(jnp.bfloat16)
    )
    top_edge = index == 0
    bottom_edge = index == count - 1
    bordered = with_halo(grid, (("tok", 0),), 1)
    bordered = clear_rows(bordered, 1, top_edge, bottom_edge)
    hidden = normalize(convolve(bordered, conv_in), gain)
    hidden = with_halo(hidden, (("tok", 0),), 1)
    hidden = clear_rows(hidden, 1, top_edge, bottom_edge)
    colours = convolve(hidden, conv_out)
    return (velocity, colours.transpose(2, 0, 1))


def contract_last(left, right):
    return lax.dot_general(
        left, right, (((1,), (1,)), ((), ())), preferred_element_type=jnp.float32
    )


def fused(
    count,
    kb_hbm, ms_hbm, guide_hbm,
    q_hbm, k_hbm, v_hbm, kt_hbm, mt_hbm, ow_hbm, lat_hbm, ci_hbm, gain_hbm, co_hbm,
    vel_out, rgb_out,
    kb_s, ms_s, guide_s, qs, ks, vs, rq, rk, rv, kt, mt, ow, vw, lat, ci, gain, co,
    act, kbias, wts, psend, precv, ext, late, wbig, vt, weave,
    local_sem, send_sem, recv_sem, send2, recv2, lat_send, lat_recv, x_send, x_recv, relay,
):
    me = lax.axis_index("tok")
    core = lax.axis_index("branch")
    other = 1 - core
    rows = q_hbm.shape[0]
    half = rows // 2
    cols = rq.shape[1]
    heads = cols // HEAD_DIM
    tokens = rows * count
    patch = lat_hbm.shape[1]
    dec = gain.shape[0]
    lat_ch = ci.shape[0] // 9
    below = lax.rem(me + count - 1, count)
    above = lax.rem(me + 1, count)
    has_low = me > 0
    has_high = me < count - 1

    plane, side = lax.div(me, 2), lax.rem(me, 2)
    beside = plane + 1 - 2 * lax.rem(plane, 2)
    opposite = plane + 2 - 4 * lax.div(plane, 2)
    mirror = 3 - plane
    middle = (plane == 1) | (plane == 2)
    near = [
        2 * opposite + side,
        2 * beside + 1 - side,
        2 * beside + side,
        2 * plane + 1 - side,
    ]
    facing = [2 * mirror + side, 2 * mirror + 1 - side]
    distant = 2 * opposite + 1 - side
    peers = facing + [distant] + near

    def span(index):
        return pl.ds(pl.multiple_of((2 * index + core) * cols, cols), cols)

    def own_rows(index):
        return pl.ds(pl.multiple_of(index * rows, rows), rows)

    ext[...] = jnp.zeros_like(ext)
    late[0] = jnp.zeros(late.shape[1:], late.dtype)
    late[2] = jnp.zeros(late.shape[1:], late.dtype)
    barrier = pltpu.get_barrier_semaphore()
    for peer in near:
        pl.semaphore_signal(barrier, inc=1, device_id={"tok": peer}, device_id_type=MESH)
    pl.semaphore_signal(barrier, inc=1, device_id={"branch": other}, device_id_type=MESH)

    @pl.when(middle)
    def _():
        for peer in facing:
            pl.semaphore_signal(barrier, inc=1, device_id={"tok": peer}, device_id_type=MESH)

    for exists, peer in ((has_low, below), (has_high, above)):

        @pl.when(exists)
        def _(peer=peer):
            pl.semaphore_signal(
                barrier, inc=1, device_id={"tok": peer, "branch": other}, device_id_type=MESH
            )

    loads = [
        pltpu.make_async_copy(q_hbm, qs, local_sem.at[0]),
        pltpu.make_async_copy(k_hbm, ks, local_sem.at[1]),
        pltpu.make_async_copy(v_hbm, vs, local_sem.at[2]),
        pltpu.make_async_copy(lat_hbm, lat, local_sem.at[3]),
        pltpu.make_async_copy(q_hbm.at[:, span(me)], rq.at[own_rows(me), :], local_sem.at[4]),
        pltpu.make_async_copy(k_hbm.at[:, span(me)], rk.at[own_rows(me), :], local_sem.at[5]),
        pltpu.make_async_copy(kt_hbm.at[:, :, span(me)], kt, local_sem.at[7]),
        pltpu.make_async_copy(mt_hbm.at[:, :, span(me)], mt, local_sem.at[8]),
        pltpu.make_async_copy(ow_hbm, ow, local_sem.at[9]),
        pltpu.make_async_copy(ci_hbm, ci, local_sem.at[10]),
        pltpu.make_async_copy(gain_hbm, gain, local_sem.at[11]),
        pltpu.make_async_copy(co_hbm, co, local_sem.at[12]),
        pltpu.make_async_copy(kb_hbm, kb_s, local_sem.at[13]),
        pltpu.make_async_copy(ms_hbm, ms_s, local_sem.at[14]),
        pltpu.make_async_copy(guide_hbm, guide_s, local_sem.at[15]),
    ]
    for load in loads:
        load.start()
    for load in loads[:4]:
        load.wait()
    late[1] = jnp.concatenate([lat[:half, :], lat[half:, :]], axis=1)

    def flag(condition):
        return jnp.where(condition, 1, 0)

    pl.semaphore_wait(barrier, 5 + 2 * flag(middle) + flag(has_low) + flag(has_high))
    pl.semaphore_signal(relay, inc=1, device_id={"tok": near[0]}, device_id_type=MESH)

    moves = ((qs, rq), (ks, rk), (vs, rv))

    def block_copy(which, at):
        source, target = moves[which]
        return pltpu.make_async_remote_copy(
            src_ref=vw.at[peers[at]] if which == 2 else source.at[:, span(peers[at])],
            dst_ref=target.at[own_rows(me), :],
            send_sem=send_sem.at[which, at],
            recv_sem=recv_sem.at[which, me],
            device_id={"tok": peers[at]},
            device_id_type=MESH,
        )

    @pl.when(middle)
    def _():
        for which in range(2):
            for at in range(2):
                block_copy(which, at).start()

    for which in range(2):
        for at in range(3, count - 1):
            block_copy(which, at).start()

    def latent_copy(peer, slot):
        return pltpu.make_async_remote_copy(
            src_ref=late.at[1],
            dst_ref=late.at[slot],
            send_sem=lat_send.at[slot],
            recv_sem=lat_recv.at[slot],
            device_id={"tok": peer},
            device_id_type=MESH,
        )

    @pl.when(has_low)
    def _():
        latent_copy(below, 2).start()

    @pl.when(has_high)
    def _():
        latent_copy(above, 0).start()

    pl.semaphore_wait(relay, 1)

    @pl.when(jnp.logical_not(middle))
    def _():
        for which in range(2):
            for at in range(2):
                block_copy(which, at).start()

    for which in range(2):
        block_copy(which, 2).start()
    for load in loads[4:]:
        load.wait()
    for index in range(count):
        block, weight = vs[:, span(index)], ow[:, span(index)]
        ahead = [
            contract_last(
                block[:, at * HEAD_DIM : (at + 1) * HEAD_DIM],
                weight[:, at * HEAD_DIM : (at + 1) * HEAD_DIM],
            )
            for at in range(heads)
        ]
        vw[index] = jnp.concatenate(ahead, axis=1).astype(vw.dtype)
    rv[own_rows(me), :] = vw[me]
    for at in range(count - 1):
        block_copy(2, at).start()
    sends = [block_copy(which, at) for which in range(3) for at in range(count - 1)]

    def arrived(which, target):
        for step, peer in enumerate(peers):
            pltpu.make_async_remote_copy(
                src_ref=target.at[own_rows(peer), :],
                dst_ref=target.at[own_rows(peer), :],
                send_sem=send_sem.at[which, step],
                recv_sem=recv_sem.at[which, peer],
                device_id={"tok": peer},
                device_id_type=MESH,
            ).wait_recv()

    for frame in range(count):
        key_rows = kt[kb_s[frame]].astype(jnp.float32)
        mouse_rows = mt[ms_s[frame]].astype(jnp.float32)
        for which, term in enumerate((key_rows + mouse_rows, mouse_rows, key_rows)):
            for part in range(2):
                act[part, which, frame : frame + 1, :] = term[part : part + 1, :]
    for which in range(3):
        spread = jnp.broadcast_to(act[0, which][:, None, :], (count, rows, cols))
        kbias[which] = spread.reshape(tokens, cols).astype(jnp.bfloat16)
    wbig[...] = jnp.zeros_like(wbig)
    for place in range(2):
        for shift in range(2):
            out_at = (place * 2 + shift) * dec
            for first in range(3):
                for second in range(3):
                    line, column = place + first, shift + second
                    second_half = column in (0, 3)
                    part = {0: 1, 1: 0, 2: 1, 3: 0}[column]
                    at = second_half * 2 * patch + line * 2 * lat_ch + part * lat_ch
                    from_at = (first * 3 + second) * lat_ch
                    wbig[at : at + lat_ch, out_at : out_at + dec] = ci[
                        from_at : from_at + lat_ch, :
                    ]
    colour_count = co.shape[1]
    spare = jnp.zeros((8 - colour_count, dec), jnp.float32)
    padded = [part for at in range(9) for part in (co[at].astype(jnp.float32), spare)]
    vt[...] = jnp.concatenate(padded, axis=0).astype(jnp.bfloat16)
    from_lane = lax.broadcasted_iota(jnp.int32, weave.shape, 0)
    to_lane = lax.broadcasted_iota(jnp.int32, weave.shape, 1)
    from_at = lax.rem(from_lane, 4 * rows)
    woven = 2 * from_at + from_lane // (4 * rows)
    weave[...] = jnp.where((woven == to_lane) & (from_at < 2 * rows), 1.0, 0.0).astype(
        jnp.bfloat16
    )

    arrived(0, rq)
    arrived(1, rk)
    factor = HEAD_DIM ** (-0.5) * math.log2(math.e)
    totals = []
    for head in range(heads):
        lanes = slice(head * HEAD_DIM, (head + 1) * HEAD_DIM)
        query = rq[:, lanes]
        key = rk[:, lanes]
        both = jnp.concatenate([query, query], axis=1)
        for which in range(4):
            if which < 3:
                scores = contract_last(
                    both, jnp.concatenate([key, kbias[which, :, lanes]], axis=1)
                )
            else:
                scores = contract_last(query, key)
            top = jnp.max(scores, axis=1, keepdims=True)
            raised = jnp.exp2((scores - top) * factor)
            totals.append(jnp.sum(raised, axis=1, keepdims=True))
            wts[head * 4 + which] = raised.astype(jnp.bfloat16)
    arrived(2, rv)
    own_weight = ow[:, span(me)]
    part_sums = None
    for head in range(heads):
        lanes = slice(head * HEAD_DIM, (head + 1) * HEAD_DIM)
        plain = rv[:, head * patch : (head + 1) * patch].astype(jnp.float32)
        plain = plain.reshape(count, rows, patch)
        by_mouse, by_key = (
            contract_last(act[1, which, :, lanes].astype(jnp.bfloat16), own_weight[:, lanes])
            for which in (1, 2)
        )
        shifts = (by_key + by_mouse, by_mouse, by_key, None)
        for which, shift in enumerate(shifts):
            value = plain if shift is None else plain + shift[:, None, :]
            value = value.reshape(tokens, patch).astype(jnp.bfloat16)
            summed = jnp.dot(wts[head * 4 + which], value, preferred_element_type=jnp.float32)
            term = guide_s[which] * (summed / totals[head * 4 + which])
            part_sums = term if part_sums is None else part_sums + term
    split = part_sums.reshape(count, 2, half, patch)
    psend[...] = jnp.concatenate([split[:, 0], split[:, 1]], axis=2).astype(psend.dtype)

    for step, peer in enumerate(peers):
        copy = pltpu.make_async_remote_copy(
            src_ref=psend.at[peer],
            dst_ref=precv.at[me],
            send_sem=send2.at[step],
            recv_sem=recv2.at[me],
            device_id={"tok": peer},
            device_id_type=MESH,
        )
        copy.start()
        sends.append(copy)
    precv[me] = psend[me]
    for step, peer in enumerate(peers):
        pltpu.make_async_remote_copy(
            src_ref=psend.at[peer],
            dst_ref=precv.at[peer],
            send_sem=send2.at[step],
            recv_sem=recv2.at[peer],
            device_id={"tok": peer},
            device_id_type=MESH,
        ).wait_recv()
    ext[1, core] = jnp.sum(precv[...].astype(jnp.float32), axis=0)

    def exchange(at, slot, where):
        return pltpu.make_async_remote_copy(
            src_ref=ext.at[1, core],
            dst_ref=ext.at[slot, core],
            send_sem=x_send.at[at],
            recv_sem=x_recv.at[slot, core],
            device_id=where,
            device_id_type=MESH,
        )

    def expect(slot, branch):
        pltpu.make_async_remote_copy(
            src_ref=ext.at[1, core],
            dst_ref=ext.at[slot, branch],
            send_sem=x_send.at[0],
            recv_sem=x_recv.at[slot, branch],
            device_id={"branch": other},
            device_id_type=MESH,
        ).wait_recv()

    low_copies = [
        exchange(1, 2, {"tok": below, "branch": core}),
        exchange(2, 2, {"tok": below, "branch": other}),
    ]
    high_copies = [
        exchange(3, 0, {"tok": above, "branch": core}),
        exchange(4, 0, {"tok": above, "branch": other}),
    ]
    across = exchange(0, 1, {"branch": other})

    @pl.when(has_low)
    def _():
        for copy in low_copies:
            copy.start()

    @pl.when(has_high)
    def _():
        for copy in high_copies:
            copy.start()

    across.start()
    expect(1, other)

    @pl.when(has_low)
    def _():
        latent_copy(below, 0).wait_recv()
        expect(0, 0)
        expect(0, 1)

    @pl.when(has_high)
    def _():
        latent_copy(above, 2).wait_recv()
        expect(2, 0)
        expect(2, 1)

    velocity = ext[:, 0] + ext[:, 1]
    vel_out[:half, :] = velocity[1][:, :patch]
    vel_out[half:, :] = velocity[1][:, patch:]
    stepped = late[...] - step_size * velocity
    stepped = stepped.astype(jnp.bfloat16).astype(jnp.float32)
    lane = lax.broadcasted_iota(jnp.int32, (half, 2 * patch), 1)
    row = lax.broadcasted_iota(jnp.int32, (rows, 2 * patch), 0)
    wide = lax.broadcasted_iota(jnp.int32, (rows, 2 * patch), 1)
    blocks = []
    for low in range(2):
        one, two = stepped[low], stepped[low + 1]
        pair = jnp.concatenate(
            [
                jnp.where(lane < patch, one, pltpu.roll(two, patch, 1)),
                jnp.where(lane < patch, pltpu.roll(one, patch, 1), two),
            ],
            axis=0,
        )
        before = jnp.where(row == 0, 0.0, pltpu.roll(pair, 1, 0))
        after = jnp.where(row == rows - 1, 0.0, pltpu.roll(pair, rows - 1, 0))
        sides = jnp.where(lax.rem(wide, 2 * lat_ch) < lat_ch, after, before)
        blocks.append(jnp.concatenate([pair, sides], axis=1))
    windows = jnp.concatenate(blocks, axis=0).astype(jnp.bfloat16)
    gained = gain[...].reshape(1, dec)
    taps = []
    for shift in range(2):
        lines = []
        for place in range(2):
            out_at = (place * 2 + shift) * dec
            features = jnp.dot(
                windows, wbig[:, out_at : out_at + dec], preferred_element_type=jnp.float32
            )
            square = jnp.mean(features * features, axis=1, keepdims=True)
            scaled = features * lax.rsqrt(square + norm_eps) * gained
            lines.append(scaled / (1.0 + jnp.exp(-scaled)))
        ordered = jnp.concatenate(
            [
                jnp.where(has_low, lines[0][:rows], 0.0),
                lines[1][:rows],
                lines[0][rows:],
                jnp.where(has_high, lines[1][rows:], 0.0),
            ],
            axis=0,
        ).astype(jnp.bfloat16)
        taps.append(contract_last(vt[...], ordered))
    inner = lax.rem(lax.broadcasted_iota(jnp.int32, (8, 4 * rows), 1), rows)

    def tap(shift, first, second):
        at = (first * 3 + second) * 8
        return taps[shift][at : at + 8, :]

    halves = []
    for shift in range(2):
        out = None
        for first in range(3):
            if shift == 0:
                edge = jnp.where(inner == 0, 0.0, pltpu.roll(tap(1, first, 0), 1, 1))
                line = tap(0, first, 1) + tap(1, first, 2) + edge
            else:
                edge = jnp.where(
                    inner == rows - 1, 0.0, pltpu.roll(tap(0, first, 2), 4 * rows - 1, 1)
                )
                line = tap(0, first, 0) + tap(1, first, 1) + edge
            if first > 0:
                line = pltpu.roll(line, (4 - first) * rows, 1)
            out = line if out is None else out + line
        halves.append(out)
    rest = jnp.concatenate(halves, axis=1)
    parts = []
    for _ in range(3):
        parts.append(rest.astype(jnp.bfloat16).astype(jnp.float32))
        rest = rest - parts[-1]
    moved = jnp.dot(
        jnp.concatenate(parts, axis=0).astype(jnp.bfloat16),
        weave[...],
        preferred_element_type=jnp.float32,
    )
    colours = moved[:8] + moved[8:16] + moved[16:]
    for line in range(2):
        rgb_out[:, line, :] = colours[:colour_count, line * 2 * rows : (line + 1) * 2 * rows]

    for copy in sends:
        copy.wait_send()
    across.wait_send()

    @pl.when(has_low)
    def _():
        latent_copy(below, 2).wait_send()
        for copy in low_copies:
            copy.wait_send()

    @pl.when(has_high)
    def _():
        latent_copy(above, 0).wait_send()
        for copy in high_copies:
            copy.wait_send()


def fused_shards(
    queries,
    keys,
    values,
    keyboard,
    mouse,
    key_table,
    mouse_table,
    guidance,
    out_weight,
    latent,
    conv_in,
    gain,
    conv_out,
):
    count = lax.axis_size("tok")
    rows, width = queries.shape
    cols = width // (2 * count)
    tokens = rows * count
    patch = latent.shape[1]
    lat_ch, dec = conv_in.shape[2:]
    colours = conv_out.shape[3]
    half = rows // 2
    bf16, f32 = jnp.bfloat16, jnp.float32
    hbm = pl.BlockSpec(memory_space=pltpu.HBM)
    vmem = pl.BlockSpec(memory_space=pltpu.VMEM)
    dma = pltpu.SemaphoreType.DMA

    def pin(array):
        return pltpu.with_memory_space_constraint(array, pltpu.HBM)

    velocity, rgb = pl.pallas_call(
        functools.partial(fused, count),
        out_shape=(
            jax.ShapeDtypeStruct((rows, patch), f32),
            jax.ShapeDtypeStruct((colours, 2, 2 * rows), f32),
        ),
        in_specs=[hbm] * 13,
        out_specs=(vmem, vmem),
        scratch_shapes=[
            pltpu.SMEM(keyboard.shape, jnp.int32),
            pltpu.SMEM(mouse.shape, jnp.int32),
            pltpu.SMEM(guidance.shape, f32),
            pltpu.VMEM((rows, width), bf16),
            pltpu.VMEM((rows, width), bf16),
            pltpu.VMEM((rows, width), bf16),
            pltpu.VMEM((tokens, cols), bf16),
            pltpu.VMEM((tokens, cols), bf16),
            pltpu.VMEM((tokens, cols // HEAD_DIM * patch), bf16),
            pltpu.VMEM((key_table.shape[0], 2, cols), bf16),
            pltpu.VMEM((mouse_table.shape[0], 2, cols), bf16),
            pltpu.VMEM((patch, width), bf16),
            pltpu.VMEM((count, rows, cols // HEAD_DIM * patch), bf16),
            pltpu.VMEM((rows, patch), f32),
            pltpu.VMEM((9 * lat_ch, dec), bf16),
            pltpu.VMEM((dec,), f32),
            pltpu.VMEM((9, colours, dec), bf16),
            pltpu.VMEM((2, 3, count, cols), f32),
            pltpu.VMEM((3, tokens, cols), bf16),
            pltpu.VMEM((4 * cols // HEAD_DIM, tokens, tokens), bf16),
            pltpu.VMEM((count, half, 2 * patch), bf16),
            pltpu.VMEM((count, half, 2 * patch), bf16),
            pltpu.VMEM((3, 2, half, 2 * patch), f32),
            pltpu.VMEM((3, half, 2 * patch), f32),
            pltpu.VMEM((4 * patch, 4 * dec), bf16),
            pltpu.VMEM((72, dec), bf16),
            pltpu.VMEM((8 * rows, 4 * rows), bf16),
            dma((16,)),
            dma((3, count)),
            dma((3, count)),
            dma((count,)),
            dma((count,)),
            dma((3,)),
            dma((3,)),
            dma((5,)),
            dma((3, 2)),
            pltpu.SemaphoreType.REGULAR,
        ],
        compiler_params=pltpu.CompilerParams(collective_id=0, has_side_effects=True, vmem_limit_bytes=16 * 2**20),
    )(
        pin(keyboard),
        pin(mouse),
        pin(guidance),
        pin(queries),
        pin(keys),
        pin(values),
        pin(key_table),
        pin(mouse_table),
        pin(out_weight.T),
        pin(latent),
        pin(conv_in.reshape(9 * lat_ch, dec)),
        pin(gain),
        pin(conv_out.transpose(0, 1, 3, 2).reshape(9, colours, dec)),
    )
    return velocity, rgb


def solution(mesh):
    placed = (
        P(("groups", "tok"), None),
        P(("groups", "tok"), None),
        P(("groups", "tok"), None),
        P("groups"),
        P("groups"),
        P(),
        P(),
        P(),
        P(),
        P(("groups", "tok"), None),
        P(),
        P(),
        P(),
    )

    def step(queries, keys, values, keyboard, *rest):
        count = lax.axis_size("tok")
        single = count == 8 and keyboard.shape[0] == count
        body = fused_shards if single else shards
        return body(queries, keys, values, keyboard, *rest)

    return jax.shard_map(
        step,
        mesh=mesh,
        in_specs=placed,
        out_specs=(P(("groups", "tok"), None), P(None, ("groups", "tok"), None)),
        check_vma=False,
    )
```
